128 devices in a mesh: ap: 32 (over y, x_hi, z), rg: 4 (over x_lo, core).
Axes of the slice: x: 4 (x_hi: 2, x_lo: 2; x = x_hi * 2 + x_lo), y: 4, z: 4, core: 2. Of those that a mesh axis runs over, the one named last changes fastest.
Arguments:
- raw_echoes: bfloat16 [2, 8192, 4096], P(None, 'ap', 'rg'), may hold values from -6 to 6
- chirp: float32 [2, 128], replicated, may hold values from -0.375 to 0.375
- range_offsets: int32 [8, 2, 4096], P(None, None, 'rg'), may hold values from 0 to 7
- phases: float32 [8, 2, 4096], P(None, None, 'rg'), may hold values from -3.140625 to 3.140625
- tile_table: int32 [1024, 16], replicated, may hold values from 0 to 16383, as said below
Outputs:
- image: float32 [2, 8192, 4096], P(None, 'ap', 'rg')
The draws below stay inside these ranges and needn't reach their ends.
Inputs may be any that keep to these rules, and one draw needn't show every extreme that they name: `tile_table`: all entries differ (a permutation of tile indices). The tiles that lie in one device's block of the image (256 pulses by 1024 range bins) go to tiles of distinct devices' blocks, one to each device. The same holds for each set of tiles whose tile rows u share one value of u mod (32) and whose columns lie in one device's range bins.
All inputs are finite; a program needn't handle non-finite values.
Results may differ from the reference program's by a relative error of at most 0.0029.
Values may be sent and summed in bfloat16 or wider, within the bound.
No kernel may reach another device: no remote copies, remote signals or barrier semaphores. Data moves between devices by JAX's collectives and lax.ppermute only.
A program may use at most 64 MiB of HBM per device.

```python
import jax
import jax.numpy as jnp
from jax import lax

R = 4096
CHIRP = 128
MERGES = 8
APER = 8192
N_AP = 32
N_RG = 4


def draw_tile_table(key, part):
    row_perm = jax.random.permutation(jax.random.fold_in(key, 11), N_AP).astype(jnp.int32)
    col_perm = jax.random.permutation(jax.random.fold_in(key, 23), N_RG).astype(jnp.int32)
    slot_perm = jax.random.permutation(jax.random.fold_in(key, 37), N_AP).astype(jnp.int32)
    bin_perm = jax.random.permutation(jax.random.fold_in(key, 41), N_RG).astype(jnp.int32)
    shifts = jax.random.randint(jax.random.fold_in(key, 53), (N_AP,), 0, N_RG).astype(jnp.int32)
    source_ap = jnp.arange(N_AP, dtype=jnp.int32)[:, None, None, None]
    inner_row = jnp.arange(N_AP, dtype=jnp.int32)[None, :, None, None]
    source_rg = jnp.arange(N_RG, dtype=jnp.int32)[None, None, :, None]
    inner_col = jnp.arange(N_RG, dtype=jnp.int32)[None, None, None, :]
    target_ap = row_perm[(source_ap + inner_row) % N_AP]
    target_rg = col_perm[(inner_col + source_rg) % N_RG]
    slot_row = slot_perm[source_ap] + 0 * inner_row + 0 * source_rg + 0 * inner_col
    slot_col = bin_perm[(source_rg + shifts[source_ap]) % N_RG] + 0 * inner_row + 0 * inner_col
    tile_row = target_ap * N_AP + slot_row
    tile_col = target_rg * N_RG + slot_col
    destination = tile_row * (N_RG * N_RG) + tile_col
    return destination.reshape(N_AP * N_AP, N_RG * N_RG).astype(jnp.int32)


def with_ends(values, stream_key, least, high):
    place = [jax.random.randint(jax.random.fold_in(stream_key, axis), (), 0, length) for axis, length in enumerate(values.shape)]
    longest = values.shape.index(max(values.shape))
    beside = place[:longest] + [(place[longest] + 1) % values.shape[longest]] + place[longest + 1:]
    return values.at[tuple(place)].set(least).at[tuple(beside)].set(high)


def levels(key, dims, pieces, smallest, high):
    factor_of, own = 1.0, jax.random.fold_in(key, 6)
    for position, shards_of in pieces:
        draws = jnp.exp(jax.random.uniform(jax.random.fold_in(own, position), (shards_of,), jnp.float32, smallest / len(pieces), high / len(pieces)))
        factor_of = factor_of * jnp.repeat(draws, dims[position] // shards_of).reshape([-1 if axis == position else 1 for axis in range(len(dims))])
    return factor_of


def gaussian(own_key, shape, scale, bound, split=(), kind=jnp.bfloat16):
    loudness = levels(own_key, shape, split, -0.22, 0.18) if split else 1.0
    array = jax.random.normal(own_key, shape, jnp.float32) * scale * loudness
    return jnp.minimum(jnp.maximum(array, -bound), bound).astype(kind)


def setup_inputs(seed: int = 0) -> dict:
    key_of = jax.random.split(jax.random.key(seed), 6)
    raw_echoes = gaussian(key_of[0], (2, APER, R), 1.0, 6.0, ((1, 32), (2, 4)))
    chirp = gaussian(key_of[1], (2, CHIRP), (2 * CHIRP) ** -0.5, 0.375, (), jnp.float32)
    range_offsets = with_ends(jax.random.randint(key_of[2], (MERGES, 2, R), 0, 8), jax.random.fold_in(key_of[2], 1), 0, 7).astype(jnp.int32)
    phases = jnp.clip(jax.random.uniform(key_of[3], (MERGES, 2, R), jnp.float32, -3.140625, 3.140625), -3.140625, 3.140625)
    tile_table = draw_tile_table(jax.random.fold_in(key_of[5], 71), 0)
    return dict(raw_echoes=raw_echoes, chirp=chirp, range_offsets=range_offsets, phases=phases, tile_table=tile_table)


root_half = 0.7071067811865476


def toeplitz_table(chirp_taps, window, block):
    tap_count = chirp_taps.shape[1]
    tap_lag = lax.broadcasted_iota(jnp.int32, (window, block), 0) - lax.broadcasted_iota(jnp.int32, (window, block), 1)
    picker = (tap_lag[:, :, None] == lax.broadcasted_iota(jnp.int32, (1, 1, tap_count), 2)).astype(jnp.float32)
    spread = jnp.einsum('wok,ck->cwo', picker, chirp_taps.astype(jnp.float32), precision=lax.Precision.HIGHEST)
    from_real = jnp.stack([spread[0], -spread[1]], axis=1)
    from_imag = jnp.stack([spread[1], spread[0]], axis=1)
    return jnp.stack([from_real, from_imag], axis=0).astype(jnp.bfloat16)


def rotated_term(padded, offsets, angles):
    range_bins = offsets.shape[-1]
    picked = jnp.zeros(padded.shape[:-1] + (range_bins,), jnp.float32)
    for shift_value in range(8):
        picked = jnp.where(offsets == shift_value, padded[..., shift_value:shift_value + range_bins], picked)
    cosine = jnp.cos(angles)
    sine_part = jnp.sin(angles)
    return jnp.stack([picked[0] * cosine - picked[1] * sine_part, picked[0] * sine_part + picked[1] * cosine])


def reference(raw_echoes, chirp, range_offsets, phases, tile_table):
    chirp_taps = chirp.astype(jnp.bfloat16)
    half_taps = CHIRP // 2
    block = min(128, R)
    window = block + CHIRP
    table = toeplitz_table(chirp_taps, window, block).astype(jnp.float32)
    padded = jnp.pad(raw_echoes, ((0, 0), (0, 0), (half_taps, half_taps)))

    def one_block(index):
        piece = lax.dynamic_slice_in_dim(padded, index * block, window, 2).astype(jnp.float32)
        return jnp.einsum('cpw,cwdo->dpo', piece, table, precision=lax.Precision.HIGHEST)

    filtered = lax.map(one_block, jnp.arange(R // block, dtype=jnp.int32))
    field = filtered.transpose(1, 2, 0, 3).reshape(2, APER, R)
    for merge_level in range(MERGES):
        distance = APER // 2 ** MERGES * 2 ** merge_level
        padded_field = jnp.pad(field, ((0, 0), (0, 0), (4, 4)))
        grouped = padded_field.reshape(2, APER // (2 * distance), 2, distance, R + 8)
        lower_term = rotated_term(grouped[:, :, 0], range_offsets[merge_level, 0], phases[merge_level, 0])
        upper_term = rotated_term(grouped[:, :, 1], range_offsets[merge_level, 1], phases[merge_level, 1])
        merged = jnp.stack([lower_term + upper_term, lower_term - upper_term], axis=2) * root_half
        field = merged.reshape(2, APER, R)
    tile_rows = APER // (N_AP * N_AP)
    tile_bins = R // (N_RG * N_RG)
    row_tiles = N_AP * N_AP
    col_tiles = N_RG * N_RG
    tiles = field.reshape(2, row_tiles, tile_rows, col_tiles, tile_bins).transpose(0, 1, 3, 2, 4)
    tiles = tiles.reshape(2, row_tiles * col_tiles, tile_rows, tile_bins)
    flat_table = tile_table.reshape(-1).astype(jnp.int32)
    inverse = jnp.zeros_like(flat_table).at[flat_table].set(jnp.arange(row_tiles * col_tiles, dtype=jnp.int32))
    placed = jnp.take(tiles, inverse, axis=1)
    placed = placed.reshape(2, row_tiles, col_tiles, tile_rows, tile_bins).transpose(0, 1, 3, 2, 4)
    return placed.reshape(2, APER, R)
```

```python
import functools
import math

import jax
import jax.numpy as jnp
from jax import lax
from jax.experimental import pallas as pl
from jax.experimental.pallas import tpu as pltpu
from jax.sharding import PartitionSpec as P

ROOT_HALF = 0.7071067811865476
LANES = 128
STEP = 8
LEAD = 64
VMEM = pltpu.VMEM
BF16 = jnp.bfloat16
F32 = jnp.float32


def whole(count):
    return [pl.BlockSpec(memory_space=VMEM)] * count


def split_three(values):
    high = values.astype(BF16)
    rest = values - high.astype(F32)
    middle = rest.astype(BF16)
    low = (rest - middle.astype(F32)).astype(BF16)
    return high, middle, low


def rim_kernel(raw_ref, offset_ref, phase_ref, left_ref, right_ref):
    pulses, width = raw_ref.shape[1], raw_ref.shape[2]
    rows = offset_ref.shape[0]
    for out_ref, start in ((left_ref, 0), (right_ref, width - LANES)):
        cut = slice(start, start + LANES)
        out_ref[:pulses] = raw_ref[0, :, cut]
        out_ref[pulses : 2 * pulses] = raw_ref[1, :, cut]
        at = 2 * pulses
        out_ref[at : at + rows] = offset_ref[:, cut].astype(F32).astype(BF16)
        for part in split_three(phase_ref[:, cut]):
            at += rows
            out_ref[at : at + rows] = part


def toeplitz_kernel(chirp_ref, table_ref):
    taps = chirp_ref[...].astype(BF16).astype(F32)
    zeros = jnp.zeros((1, LANES), F32)
    rolled = []
    for part in range(2):
        row = jnp.concatenate([taps[part : part + 1], zeros], axis=1)
        spread = jnp.broadcast_to(row, (LANES, 2 * LANES))
        rolled.append(pltpu.roll(spread, 0, 1, stride=1, stride_axis=0))
    real, imag = rolled
    table_ref[0] = jnp.concatenate([real, -imag], axis=0).astype(BF16)
    table_ref[1] = jnp.concatenate([imag, real], axis=0).astype(BF16)


def steering_kernel(total, offset_ref, phase_ref, left_ref, right_ref, trig_ref, index_ref):
    rows, width = offset_ref.shape
    columns = index_ref.shape[1]
    base = left_ref.shape[0] - 4 * rows
    start = lax.axis_index("rg") * width - LANES

    def rim(ref):
        parts = [
            ref[base + k * rows : base + (k + 1) * rows, :].astype(F32) for k in range(4)
        ]
        return parts[0].astype(jnp.int32), parts[1] + parts[2] + parts[3]

    left_offset, left_phase = rim(left_ref)
    right_offset, right_phase = rim(right_ref)
    offsets = jnp.concatenate([left_offset, offset_ref[...], right_offset], axis=1)
    angles = jnp.concatenate([left_phase, phase_ref[...], right_phase], axis=1)
    padded = width + 2 * LANES
    bins = start + lax.broadcasted_iota(jnp.int32, (rows, padded), 1)
    inside = (bins >= 0) & (bins < total)
    cosine = jnp.where(inside, jnp.cos(angles) * ROOT_HALF, 0.0)
    sine = jnp.where(inside, jnp.sin(angles) * ROOT_HALF, 0.0)
    lane = lax.broadcasted_iota(jnp.int32, (2, columns), 1) % LANES
    for level in range(rows // 2):
        shift = padded - (LANES - LEAD + STEP * (level + 1))
        pick = slice(2 * level, 2 * level + 2)

        def moved(values):
            return pltpu.roll(values, shift, 1)[pick, :columns]

        trig_ref[0, pick] = moved(cosine)
        trig_ref[1, pick] = moved(sine)
        index_ref[pick] = lane + (STEP - 4) + moved(offsets)


def row_of(ref, lead, row, lanes, rows):
    return jnp.broadcast_to(ref[lead + (slice(row, row + 1), lanes)], (rows, LANES))


def steering(trig_ref, index_ref, level, lanes, rows):
    sides = []
    for side in range(2):
        row = 2 * level + side
        index = row_of(index_ref, (), row, lanes, rows)
        sides.append(
            (
                index & (LANES - 1),
                index >= LANES,
                row_of(trig_ref, (0,), row, lanes, rows),
                row_of(trig_ref, (1,), row, lanes, rows),
            )
        )
    return sides


def gathered(values, index):
    return jnp.take_along_axis(values, index, axis=1, mode="promise_in_bounds")


def term_of(here, following, side):
    index, beyond, cosine, sine = side
    real, imag = (
        jnp.where(beyond, gathered(b, index), gathered(a, index))
        for a, b in zip(here, following)
    )
    return real * cosine - imag * sine, real * sine + imag * cosine


def first_merges_kernel(
    levels, total, raw_ref, left_ref, right_ref, table_ref, trig_ref, index_ref, out_ref, field_ref
):
    pulses, width = raw_ref.shape[1], raw_ref.shape[2]
    blocks = out_ref.shape[2] // LANES
    start = lax.axis_index("rg") * width - LEAD
    dims = (((1,), (1,)), ((), ()))
    for block in range(blocks):
        parts = []
        for part in range(2):
            tiles = []
            for tile in (block, block + 1):
                if tile == 0:
                    tiles.append(left_ref[part * pulses : (part + 1) * pulses, :])
                elif tile == blocks:
                    tiles.append(right_ref[part * pulses : (part + 1) * pulses, :])
                else:
                    tiles.append(raw_ref[part, :, (tile - 1) * LANES : tile * LANES])
            parts.append(
                lax.dot_general(
                    jnp.concatenate(tiles, axis=1),
                    table_ref[part],
                    dims,
                    preferred_element_type=F32,
                )
            )
        both = parts[0] + parts[1]
        if block in (0, blocks - 1):
            bins = start + block * LANES + (
                lax.broadcasted_iota(jnp.int32, both.shape, 1) % LANES
            )
            both = jnp.where((bins >= 0) & (bins < total), both, 0.0)
        lanes = slice(block * LANES, (block + 1) * LANES)
        field_ref[0, :, lanes] = both[:, :LANES]
        field_ref[1, :, lanes] = both[:, LANES:]
    for part in range(2):
        field_ref[part, :, blocks * LANES :] = jnp.zeros((pulses, LANES), F32)

    chunk = 16
    for level in range(levels):
        distance = (pulses >> levels) << level
        last = level == levels - 1

        def merge_block(block, carry, level=level, distance=distance, last=last):
            at = pl.multiple_of(block * LANES, LANES)
            lanes = pl.ds(at, LANES)
            beyond = pl.ds(pl.multiple_of(at + LANES, LANES), LANES)
            sides = steering(trig_ref, index_ref, level, lanes, chunk)
            for first in range(0, pulses, chunk):
                if first & distance:
                    continue
                terms = []
                for side in range(2):
                    rows = pl.ds(first + side * distance, chunk)
                    here = [field_ref[part, rows, lanes] for part in range(2)]
                    following = [field_ref[part, rows, beyond] for part in range(2)]
                    terms.append(term_of(here, following, sides[side]))
                for side in range(2):
                    row = first + side * distance
                    merged = [
                        terms[0][part] + terms[1][part]
                        if side == 0
                        else terms[0][part] - terms[1][part]
                        for part in range(2)
                    ]
                    if last:
                        for tile in range(chunk // 8):
                            cut = slice(tile * 8, tile * 8 + 8)
                            out_ref[row // 8 + tile, :, lanes] = jnp.concatenate(
                                [merged[0][cut], merged[1][cut]], axis=0
                            ).astype(BF16)
                    else:
                        for part in range(2):
                            field_ref[part, pl.ds(row, chunk), lanes] = merged[part]
            return carry

        lax.fori_loop(0, blocks, merge_block, 0)


def last_merges_kernel(
    skipped, target_ref, moved_ref, trig_ref, index_ref, out_ref, field_ref
):
    holders, _, columns = moved_ref.shape
    blocks = columns // LANES
    out_blocks = out_ref.shape[0] // holders * out_ref.shape[2] // LANES
    per_tile = out_ref.shape[2] // LANES
    tiles_across = out_blocks // per_tile
    levels = holders.bit_length() - 1
    for holder in range(holders):
        field_ref[holder, :, blocks * LANES :] = jnp.zeros((16, LANES), F32)
        for block in range(blocks):
            lanes = slice(block * LANES, (block + 1) * LANES)
            field_ref[holder, :, lanes] = moved_ref[holder, :, lanes].astype(F32)

    for level in range(levels):
        distance = 1 << level
        last = level == levels - 1

        def merge_block(block, carry, level=level, distance=distance, last=last):
            at = pl.multiple_of(block * LANES, LANES)
            lanes = pl.ds(at, LANES)
            beyond = pl.ds(pl.multiple_of(at + LANES, LANES), LANES)
            sides = steering(trig_ref, index_ref, skipped + level, lanes, 8)
            for first in range(holders):
                if first & distance:
                    continue
                terms = []
                for side in range(2):
                    holder = first + side * distance
                    here = [field_ref[holder, 8 * part : 8 * part + 8, lanes] for part in range(2)]
                    following = [
                        field_ref[holder, 8 * part : 8 * part + 8, beyond] for part in range(2)
                    ]
                    terms.append(term_of(here, following, sides[side]))
                for side in range(2):
                    holder = first + side * distance
                    merged = jnp.concatenate(
                        [
                            terms[0][part] + terms[1][part]
                            if side == 0
                            else terms[0][part] - terms[1][part]
                            for part in range(2)
                        ],
                        axis=0,
                    )
                    if last:
                        to = target_ref[holder * tiles_across + block // per_tile]
                        inner = pl.multiple_of(block % per_tile * LANES, LANES)
                        out_ref[to, :, pl.ds(inner, LANES)] = merged.astype(BF16)
                    else:
                        field_ref[holder, :, lanes] = merged
            return carry

        lax.fori_loop(0, out_blocks if last else blocks, merge_block, 0)


def place_kernel(source_ref, incoming_ref, out_ref):
    rows = out_ref.shape[1]
    tile_bins = incoming_ref.shape[2]
    across = out_ref.shape[2] // tile_bins
    base = pl.program_id(0) * (rows // 8) * across
    for row in range(rows // 8):
        for column in range(across):
            tile = incoming_ref[source_ref[base + row * across + column]].astype(F32)
            for part in range(2):
                out_ref[
                    part, row * 8 : row * 8 + 8, column * tile_bins : (column + 1) * tile_bins
                ] = tile[8 * part : 8 * part + 8]


def per_device(raw_echoes, chirp, range_offsets, phases, tile_table):
    ap_count, rg_count = lax.axis_size("ap"), lax.axis_size("rg")
    devices = ap_count * rg_count
    _, pulses, width = raw_echoes.shape
    level_count = range_offsets.shape[0]
    total = width * rg_count
    outer_levels = ap_count.bit_length() - 1
    inner_levels = level_count - outer_levels
    padded = width + 2 * LANES
    columns = width + LANES
    tile_rows = pulses // ap_count
    tile_bins = width // rg_count
    offset_rows = range_offsets.reshape(2 * level_count, width)
    phase_rows = phases.reshape(2 * level_count, width)
    rim_rows = 2 * pulses + 8 * level_count
    shape = jax.ShapeDtypeStruct

    to_left, to_right = pl.pallas_call(
        rim_kernel,
        out_shape=[shape((rim_rows, LANES), BF16)] * 2,
        in_specs=whole(3),
        out_specs=whole(2),
    )(raw_echoes, offset_rows, phase_rows)
    ends = rg_count - 1
    from_left = lax.ppermute(to_right, "rg", [(i, i + 1) for i in range(ends)])
    from_right = lax.ppermute(to_left, "rg", [(i + 1, i) for i in range(ends)])
    table = pl.pallas_call(
        toeplitz_kernel,
        out_shape=shape((2, 2 * LANES, 2 * LANES), BF16),
        in_specs=whole(1),
        out_specs=whole(1)[0],
    )(chirp)
    trig, index = pl.pallas_call(
        functools.partial(steering_kernel, total),
        out_shape=[
            shape((2, 2 * level_count, columns), F32),
            shape((2 * level_count, columns), jnp.int32),
        ],
        in_specs=whole(4),
        out_specs=whole(2),
    )(offset_rows, phase_rows, from_left, from_right)
    merged = pl.pallas_call(
        functools.partial(first_merges_kernel, inner_levels, total),
        out_shape=shape((ap_count, 2 * tile_rows, columns), BF16),
        in_specs=whole(6),
        out_specs=whole(1)[0],
        scratch_shapes=[VMEM((2, pulses, padded), F32)],
    )(raw_echoes, from_left, from_right, table, trig, index)
    moved = lax.all_to_all(merged, "ap", split_axis=0, concat_axis=0, tiled=True)

    ap_here, rg_here = lax.axis_index("ap"), lax.axis_index("rg")
    slot_row = tile_table // (rg_count * rg_count)
    slot_col = tile_table % (rg_count * rg_count)
    target = slot_row // ap_count * rg_count + slot_col // rg_count
    shaped = (ap_count, ap_count, rg_count, rg_count)
    target = target.reshape(shaped)
    local_slot = (slot_row % ap_count * rg_count + slot_col % rg_count).reshape(shaped)
    mine = target == ap_here * rg_count + rg_here
    slot_from = jnp.sum(jnp.where(mine, local_slot, 0), axis=(0, 3)).reshape(devices)
    ids = jnp.arange(devices, dtype=jnp.int32)
    source = jnp.sum(
        jnp.where(slot_from[None, :] == ids[:, None], ids[None, :], 0), axis=1
    )
    send_to = lax.dynamic_slice(
        target, (0, ap_here, rg_here, 0), (ap_count, 1, 1, rg_count)
    ).reshape(devices)

    outgoing = pl.pallas_call(
        functools.partial(last_merges_kernel, inner_levels),
        out_shape=shape((devices, 2 * tile_rows, tile_bins), BF16),
        grid_spec=pltpu.PrefetchScalarGridSpec(
            num_scalar_prefetch=1,
            in_specs=whole(3),
            out_specs=whole(1)[0],
            scratch_shapes=[VMEM((ap_count, 2 * tile_rows, padded), F32)],
        ),
    )(send_to, moved, trig, index)
    incoming = lax.all_to_all(outgoing, ("ap", "rg"), split_axis=0, concat_axis=0, tiled=True)
    steps = 8
    return pl.pallas_call(
        place_kernel,
        out_shape=shape((2, pulses, width), F32),
        grid_spec=pltpu.PrefetchScalarGridSpec(
            num_scalar_prefetch=1,
            grid=(steps,),
            in_specs=whole(1),
            out_specs=pl.BlockSpec((2, pulses // steps, width), lambda i, s: (0, i, 0)),
        ),
    )(source, incoming)


def solution(mesh):
    placed = (P(None, "ap", "rg"), P(), P(None, None, "rg"), P(None, None, "rg"), P())
    return jax.shard_map(
        per_device, mesh=mesh, in_specs=placed, out_specs=P(None, "ap", "rg"), check_vma=False
    )
```

```python
import functools
import math

import jax
import jax.numpy as jnp
from jax import lax
from jax.experimental import pallas as pl
from jax.experimental.pallas import tpu as pltpu
from jax.sharding import PartitionSpec as P

ROOT_HALF = 0.7071067811865476
LANES = 128
STEP = 8
LEAD = 64
VMEM = pltpu.VMEM
BF16 = jnp.bfloat16
F32 = jnp.float32


def whole(count):
    return [pl.BlockSpec(memory_space=VMEM)] * count


def at_block(block):
    return pl.ds(pl.multiple_of(block * LANES, LANES), LANES)


def split_three(values):
    high = values.astype(BF16)
    rest = values - high.astype(F32)
    middle = rest.astype(BF16)
    low = (rest - middle.astype(F32)).astype(BF16)
    return high, middle, low


def rim_kernel(head_ref, tail_ref, offset_ref, phase_ref, left_ref, right_ref):
    pulses = head_ref.shape[1]
    levels, _, width = offset_ref.shape
    rows = 2 * levels
    for edge_ref, out_ref, start in ((head_ref, left_ref, 0), (tail_ref, right_ref, width - LANES)):
        cut = slice(start, start + LANES)
        out_ref[:pulses] = edge_ref[0]
        out_ref[pulses : 2 * pulses] = edge_ref[1]
        at = 2 * pulses
        offsets = jnp.concatenate([offset_ref[l, :, cut] for l in range(levels)], axis=0)
        angles = jnp.concatenate([phase_ref[l, :, cut] for l in range(levels)], axis=0)
        out_ref[at : at + rows] = offsets.astype(F32).astype(BF16)
        for part in split_three(angles):
            at += rows
            out_ref[at : at + rows] = part


def toeplitz_kernel(chirp_ref, table_ref):
    taps = chirp_ref[...].astype(BF16).astype(F32)
    zeros = jnp.zeros((1, LANES), F32)
    rolled = []
    for part in range(2):
        row = jnp.concatenate([taps[part : part + 1], zeros], axis=1)
        spread = jnp.broadcast_to(row, (LANES, 2 * LANES))
        rolled.append(pltpu.roll(spread, 0, 1, stride=1, stride_axis=0))
    real, imag = rolled
    table_ref[0] = jnp.concatenate([real, -imag], axis=0).astype(BF16)
    table_ref[1] = jnp.concatenate([imag, real], axis=0).astype(BF16)


def gathered(values, index):
    return jnp.take_along_axis(values, index, axis=1, mode="promise_in_bounds")


def picked(here, following, index, beyond):
    return jnp.where(beyond, gathered(following, index), gathered(here, index))


def steer(levels, total, offset_ref, phase_ref, left_ref, right_ref, rows_ref, pair_refs, index_ref, trig_ref):
    all_levels, _, width = offset_ref.shape
    columns = rows_ref.shape[2]
    blocks = columns // LANES
    rim_rows = 2 * all_levels
    base = left_ref.shape[0] - 4 * rim_rows
    first, count = levels[0], 2 * len(levels)
    start = lax.axis_index("rg") * width - LANES

    def rim(ref):
        aligned = first * 2 // 16 * 16
        parts = [
            ref[base + k * rim_rows + aligned : base + (k + 1) * rim_rows, :].astype(F32)[
                2 * first - aligned : 2 * first - aligned + count
            ]
            for k in range(4)
        ]
        return parts[0], parts[1] + parts[2] + parts[3]

    left_offset, left_phase = rim(left_ref)
    right_offset, right_phase = rim(right_ref)
    middle_offset = jnp.concatenate([offset_ref[l] for l in levels], axis=0).astype(F32)
    middle_phase = jnp.concatenate([phase_ref[l] for l in levels], axis=0)
    offsets = jnp.concatenate([left_offset, middle_offset, right_offset], axis=1)
    angles = jnp.concatenate([left_phase, middle_phase, right_phase], axis=1)
    padded = width + 2 * LANES
    bins = start + lax.broadcasted_iota(jnp.int32, (count, padded), 1)
    inside = (bins >= 0) & (bins < total)
    cosine = jnp.where(inside, jnp.cos(angles) * ROOT_HALF, 0.0)
    sine = jnp.where(inside, jnp.sin(angles) * ROOT_HALF, 0.0)
    for at, level in enumerate(levels):
        shift = padded - (LANES - LEAD + STEP * (level + 1))
        pick = slice(2 * at, 2 * at + 2)
        for part, values in enumerate((offsets + (STEP - 4.0), cosine, sine)):
            rows_ref[part, pick] = pltpu.roll(values, shift, 1)[pick, :columns]

    lane = lax.broadcasted_iota(jnp.int32, (8, LANES), 1)
    for at in range(1, len(levels)):
        inner = 1 << at
        group = max(inner, 8)
        source, target = pair_refs[(at + 1) % 2], pair_refs[at % 2]
        last = at == len(levels) - 1
        for block in range(index_ref.shape[1] // LANES if last else blocks):
            lanes = slice(block * LANES, (block + 1) * LANES)
            ahead = min(block + 1, blocks - 1)
            beyond_lanes = slice(ahead * LANES, (ahead + 1) * LANES)

            def load(part, where):
                if at == 1:
                    return jnp.broadcast_to(
                        jnp.concatenate([rows_ref[part, 0:2, where]] * 4, axis=0), (8, LANES)
                    )
                return source[part, :group, where]

            for side in range(2):
                row = 2 * at + side
                step = jnp.broadcast_to(rows_ref[0, row : row + 1, lanes], (8, LANES))
                cos_out = jnp.broadcast_to(rows_ref[1, row : row + 1, lanes], (8, LANES))
                sin_out = jnp.broadcast_to(rows_ref[2, row : row + 1, lanes], (8, LANES))
                index = lane + step.astype(jnp.int32)
                beyond = index >= LANES
                index = index & (LANES - 1)
                for sub in range(group // 8):
                    cut = slice(8 * sub, 8 * sub + 8)
                    moved, cos_in, sin_in = (
                        picked(
                            load(part, lanes)[cut], load(part, beyond_lanes)[cut], index, beyond
                        )
                        for part in range(3)
                    )
                    real = cos_out * cos_in - sin_out * sin_in
                    imag = cos_out * sin_in + sin_out * cos_in
                    moved = moved + step
                    used = min(inner, 8)
                    rows = slice(side * inner + 8 * sub, side * inner + 8 * sub + used)
                    if last:
                        index_ref[rows, lanes] = (lane + moved.astype(jnp.int32))[:used]
                        trig_ref[0, rows, lanes] = real[:used]
                        trig_ref[1, rows, lanes] = imag[:used]
                    else:
                        target[0, rows, lanes] = moved[:used]
                        target[1, rows, lanes] = real[:used]
                        target[2, rows, lanes] = imag[:used]


def steer_kernel(levels, total, offset_ref, phase_ref, left_ref, right_ref, index_ref, trig_ref, rows_ref, even_ref, odd_ref):
    steer(
        levels,
        total,
        offset_ref,
        phase_ref,
        left_ref,
        right_ref,
        rows_ref,
        (even_ref, odd_ref),
        index_ref,
        trig_ref,
    )


def steer_scratch(count, columns):
    rows = max(8, 1 << (count - 1))
    return [VMEM((3, 2 * count, columns), F32)] + [VMEM((3, rows, columns), F32)] * 2


def combination(index_ref, trig_ref, row, lanes, rows):
    def spread(values):
        return jnp.broadcast_to(values, (rows, LANES))

    index = spread(index_ref[row : row + 1, lanes])
    cosine = spread(trig_ref[0, row : row + 1, lanes])
    sine = spread(trig_ref[1, row : row + 1, lanes])
    return index & (LANES - 1), index >= LANES, cosine, sine


def term_of(here, following, steering):
    index, beyond, cosine, sine = steering
    real, imag = (picked(a, b, index, beyond) for a, b in zip(here, following))
    return real * cosine - imag * sine, real * sine + imag * cosine


def sums_and_differences(values):
    values = list(values)
    distance = 1
    while distance < len(values):
        for at in range(len(values)):
            if not at & distance:
                low, high = values[at], values[at + distance]
                values[at], values[at + distance] = low + high, low - high
        distance *= 2
    return values


def first_merges_kernel(
    levels,
    total,
    raw_ref,
    left_ref,
    right_ref,
    table_ref,
    offset_ref,
    phase_ref,
    out_ref,
    field_ref,
    term_ref,
    index_ref,
    trig_ref,
    rows_ref,
    even_ref,
    odd_ref,
):
    pulses, width = raw_ref.shape[1], raw_ref.shape[2]
    blocks = out_ref.shape[2] // LANES
    start = lax.axis_index("rg") * width - LEAD
    dims = (((1,), (1,)), ((), ()))
    for block in range(blocks):
        parts = []
        for part in range(2):
            tiles = []
            for tile in (block, block + 1):
                if tile == 0:
                    tiles.append(left_ref[part * pulses : (part + 1) * pulses, :])
                elif tile == blocks:
                    tiles.append(right_ref[part * pulses : (part + 1) * pulses, :])
                else:
                    tiles.append(raw_ref[part, :, (tile - 1) * LANES : tile * LANES])
            parts.append(
                lax.dot_general(
                    jnp.concatenate(tiles, axis=1),
                    table_ref[part],
                    dims,
                    preferred_element_type=F32,
                )
            )
        both = parts[0] + parts[1]
        if block in (0, blocks - 1):
            bins = start + block * LANES + (
                lax.broadcasted_iota(jnp.int32, both.shape, 1) % LANES
            )
            both = jnp.where((bins >= 0) & (bins < total), both, 0.0)
        lanes = slice(block * LANES, (block + 1) * LANES)
        field_ref[0, :, lanes] = both[:, :LANES]
        field_ref[1, :, lanes] = both[:, LANES:]
    steer(
        range(levels),
        total,
        offset_ref,
        phase_ref,
        left_ref,
        right_ref,
        rows_ref,
        (even_ref, odd_ref),
        index_ref,
        trig_ref,
    )
    combinations = 1 << levels
    chunk = pulses // combinations

    def merge_block(block, carry):
        lanes = at_block(block)
        beyond = at_block(jnp.minimum(block + 1, blocks - 1))
        for at in range(combinations):
            steering = combination(index_ref, trig_ref, at, lanes, chunk)
            rows = slice(at * chunk, (at + 1) * chunk)
            here = [field_ref[part, rows, lanes] for part in range(2)]
            following = [field_ref[part, rows, beyond] for part in range(2)]
            term_ref[0, at], term_ref[1, at] = term_of(here, following, steering)
        for tile in range(chunk // 8):
            cut = slice(8 * tile, 8 * tile + 8)
            real, imag = (
                sums_and_differences([term_ref[part, at, cut] for at in range(combinations)])
                for part in range(2)
            )
            for at in range(combinations):
                out_ref[at * (chunk // 8) + tile, :, lanes] = jnp.concatenate(
                    [real[at], imag[at]], axis=0
                ).astype(BF16)
        return carry

    lax.fori_loop(0, blocks, merge_block, 0)


def last_merges_kernel(target_ref, moved_ref, index_ref, trig_ref, out_ref, term_ref):
    holders, _, columns = moved_ref.shape
    per_tile = out_ref.shape[2] // LANES
    out_blocks = out_ref.shape[0] // holders * per_tile
    tiles_across = out_blocks // per_tile

    def merge_block(block, carry):
        lanes = at_block(block)
        beyond = at_block(block + 1)
        for at in range(holders):
            steering = combination(index_ref, trig_ref, at, lanes, 8)
            here = moved_ref[at, :, lanes].astype(F32)
            following = moved_ref[at, :, beyond].astype(F32)
            term_ref[0, at], term_ref[1, at] = term_of(
                (here[:8], here[8:]), (following[:8], following[8:]), steering
            )
        real, imag = (
            sums_and_differences([term_ref[part, at] for at in range(holders)])
            for part in range(2)
        )
        inner = at_block(block % per_tile)
        for at in range(holders):
            to = target_ref[at * tiles_across + block // per_tile]
            out_ref[to, :, inner] = jnp.concatenate([real[at], imag[at]], axis=0).astype(BF16)
        return carry

    lax.fori_loop(0, out_blocks, merge_block, 0)


def place_kernel(source_ref, incoming_ref, out_ref):
    rows = out_ref.shape[1]
    tile_bins = incoming_ref.shape[2]
    across = out_ref.shape[2] // tile_bins
    base = pl.program_id(0) * (rows // 8) * across
    for row in range(rows // 8):
        for column in range(across):
            tile = incoming_ref[source_ref[base + row * across + column]].astype(F32)
            for part in range(2):
                out_ref[
                    part, row * 8 : row * 8 + 8, column * tile_bins : (column + 1) * tile_bins
                ] = tile[8 * part : 8 * part + 8]


def per_device(raw_echoes, chirp, range_offsets, phases, tile_table):
    ap_count, rg_count = lax.axis_size("ap"), lax.axis_size("rg")
    devices = ap_count * rg_count
    _, pulses, width = raw_echoes.shape
    level_count = range_offsets.shape[0]
    total = width * rg_count
    outer_levels = ap_count.bit_length() - 1
    inner_levels = level_count - outer_levels
    columns = width + LANES
    tile_rows = pulses // ap_count
    tile_bins = width // rg_count
    rim_rows = 2 * pulses + 8 * level_count
    shape = jax.ShapeDtypeStruct

    edge = (2, pulses, LANES)
    last_edge = width // LANES - 1
    to_left, to_right = pl.pallas_call(
        rim_kernel,
        grid=(1,),
        out_shape=[shape((rim_rows, LANES), BF16)] * 2,
        in_specs=[
            pl.BlockSpec(edge, lambda i: (0, 0, 0)),
            pl.BlockSpec(edge, lambda i: (0, 0, last_edge)),
        ]
        + whole(2),
        out_specs=whole(2),
    )(raw_echoes, raw_echoes, range_offsets, phases)
    ends = rg_count - 1
    from_left = lax.ppermute(to_right, "rg", [(i, i + 1) for i in range(ends)])
    from_right = lax.ppermute(to_left, "rg", [(i + 1, i) for i in range(ends)])
    table = pl.pallas_call(
        toeplitz_kernel,
        out_shape=shape((2, 2 * LANES, 2 * LANES), BF16),
        in_specs=whole(1),
        out_specs=whole(1)[0],
    )(chirp)
    inner = 1 << inner_levels
    merged = pl.pallas_call(
        functools.partial(first_merges_kernel, inner_levels, total),
        out_shape=shape((ap_count, 2 * tile_rows, columns), BF16),
        in_specs=whole(6),
        out_specs=whole(1)[0],
        scratch_shapes=[
            VMEM((2, pulses, columns), F32),
            VMEM((2, inner, pulses // inner, LANES), F32),
            VMEM((inner, columns), jnp.int32),
            VMEM((2, inner, columns), F32),
        ]
        + steer_scratch(inner_levels, columns),
    )(raw_echoes, from_left, from_right, table, range_offsets, phases)
    moved = lax.all_to_all(merged, "ap", split_axis=0, concat_axis=0, tiled=True)
    index, trig = pl.pallas_call(
        functools.partial(steer_kernel, range(inner_levels, level_count), total),
        out_shape=[shape((ap_count, width), jnp.int32), shape((2, ap_count, width), F32)],
        in_specs=whole(4),
        out_specs=whole(2),
        scratch_shapes=steer_scratch(outer_levels, columns),
    )(range_offsets, phases, from_left, from_right)

    ap_here, rg_here = lax.axis_index("ap"), lax.axis_index("rg")
    slot_row = tile_table // (rg_count * rg_count)
    slot_col = tile_table % (rg_count * rg_count)
    target = slot_row // ap_count * rg_count + slot_col // rg_count
    shaped = (ap_count, ap_count, rg_count, rg_count)
    target = target.reshape(shaped)
    local_slot = (slot_row % ap_count * rg_count + slot_col % rg_count).reshape(shaped)
    mine = target == ap_here * rg_count + rg_here
    slot_from = jnp.sum(jnp.where(mine, local_slot, 0), axis=(0, 3)).reshape(devices)
    ids = jnp.arange(devices, dtype=jnp.int32)
    source = jnp.sum(
        jnp.where(slot_from[None, :] == ids[:, None], ids[None, :], 0), axis=1
    )
    send_to = lax.dynamic_slice(
        target, (0, ap_here, rg_here, 0), (ap_count, 1, 1, rg_count)
    ).reshape(devices)

    outgoing = pl.pallas_call(
        last_merges_kernel,
        out_shape=shape((devices, 2 * tile_rows, tile_bins), BF16),
        grid_spec=pltpu.PrefetchScalarGridSpec(
            num_scalar_prefetch=1,
            in_specs=whole(3),
            out_specs=whole(1)[0],
            scratch_shapes=[VMEM((2, ap_count, tile_rows, LANES), F32)],
        ),
    )(send_to, moved, index, trig)
    incoming = lax.all_to_all(outgoing, ("ap", "rg"), split_axis=0, concat_axis=0, tiled=True)
    steps = 8
    return pl.pallas_call(
        place_kernel,
        out_shape=shape((2, pulses, width), F32),
        grid_spec=pltpu.PrefetchScalarGridSpec(
            num_scalar_prefetch=1,
            grid=(steps,),
            in_specs=whole(1),
            out_specs=pl.BlockSpec((2, pulses // steps, width), lambda i, s: (0, i, 0)),
        ),
    )(source, incoming)


def solution(mesh):
    placed = (P(None, "ap", "rg"), P(), P(None, None, "rg"), P(None, None, "rg"), P())
    return jax.shard_map(
        per_device, mesh=mesh, in_specs=placed, out_specs=P(None, "ap", "rg"), check_vma=False
    )
```

```python
import functools
import math

import jax
import jax.numpy as jnp
from jax import lax
from jax.experimental import pallas as pl
from jax.experimental.pallas import tpu as pltpu
from jax.sharding import PartitionSpec as P

ROOT_HALF = 0.7071067811865476
LANES = 128
STEP = 8
LEAD = 64
VMEM = pltpu.VMEM
BF16 = jnp.bfloat16
F32 = jnp.float32


def whole(count):
    return [pl.BlockSpec(memory_space=VMEM)] * count


def near(value):
    return pltpu.with_memory_space_constraint(value, VMEM)


def params():
    return pltpu.CompilerParams(vmem_limit_bytes=24 * 2**20)


def at_block(block):
    return pl.ds(pl.multiple_of(block * LANES, LANES), LANES)


def split_three(values):
    high = values.astype(BF16)
    rest = values - high.astype(F32)
    middle = rest.astype(BF16)
    low = (rest - middle.astype(F32)).astype(BF16)
    return high, middle, low


def rim_kernel(head_ref, tail_ref, offset_ref, phase_ref, left_ref, right_ref):
    pulses = head_ref.shape[1]
    levels, _, width = offset_ref.shape
    rows = 2 * levels
    for edge_ref, out_ref, start in ((head_ref, left_ref, 0), (tail_ref, right_ref, width - LANES)):
        cut = slice(start, start + LANES)
        out_ref[:pulses] = edge_ref[0]
        out_ref[pulses : 2 * pulses] = edge_ref[1]
        at = 2 * pulses
        offsets = jnp.concatenate([offset_ref[l, :, cut] for l in range(levels)], axis=0)
        angles = jnp.concatenate([phase_ref[l, :, cut] for l in range(levels)], axis=0)
        out_ref[at : at + rows] = offsets.astype(F32).astype(BF16)
        for part in split_three(angles):
            at += rows
            out_ref[at : at + rows] = part


def toeplitz_kernel(chirp_ref, table_ref):
    taps = chirp_ref[...].astype(BF16).astype(F32)
    zeros = jnp.zeros((1, LANES), F32)
    rolled = []
    for part in range(2):
        row = jnp.concatenate([taps[part : part + 1], zeros], axis=1)
        spread = jnp.broadcast_to(row, (LANES, 2 * LANES))
        rolled.append(pltpu.roll(spread, 0, 1, stride=1, stride_axis=0))
    real, imag = rolled
    table_ref[0] = jnp.concatenate([real, -imag], axis=0).astype(BF16)
    table_ref[1] = jnp.concatenate([imag, real], axis=0).astype(BF16)


def gathered(values, index):
    return jnp.take_along_axis(values, index, axis=1, mode="promise_in_bounds")


def picked(here, following, index, beyond):
    return jnp.where(beyond, gathered(following, index), gathered(here, index))


def steer(levels, total, offset_ref, phase_ref, left_ref, right_ref, rows_ref, pair_refs, index_ref, trig_ref):
    all_levels, _, width = offset_ref.shape
    columns = rows_ref.shape[2]
    blocks = columns // LANES
    rim_rows = 2 * all_levels
    base = left_ref.shape[0] - 4 * rim_rows
    first, count = levels[0], 2 * len(levels)
    start = lax.axis_index("rg") * width - LANES

    def rim(ref):
        aligned = first * 2 // 16 * 16
        parts = [
            ref[base + k * rim_rows + aligned : base + (k + 1) * rim_rows, :].astype(F32)[
                2 * first - aligned : 2 * first - aligned + count
            ]
            for k in range(4)
        ]
        return parts[0], parts[1] + parts[2] + parts[3]

    left_offset, left_phase = rim(left_ref)
    right_offset, right_phase = rim(right_ref)
    middle_offset = jnp.concatenate([offset_ref[l] for l in levels], axis=0).astype(F32)
    middle_phase = jnp.concatenate([phase_ref[l] for l in levels], axis=0)
    offsets = jnp.concatenate([left_offset, middle_offset, right_offset], axis=1)
    angles = jnp.concatenate([left_phase, middle_phase, right_phase], axis=1)
    padded = width + 2 * LANES
    bins = start + lax.broadcasted_iota(jnp.int32, (count, padded), 1)
    inside = (bins >= 0) & (bins < total)
    cosine = jnp.where(inside, jnp.cos(angles) * ROOT_HALF, 0.0)
    sine = jnp.where(inside, jnp.sin(angles) * ROOT_HALF, 0.0)
    for at, level in enumerate(levels):
        shift = padded - (LANES - LEAD + STEP * (level + 1))
        pick = slice(2 * at, 2 * at + 2)
        for part, values in enumerate((offsets + (STEP - 4.0), cosine, sine)):
            rows_ref[part, pick] = pltpu.roll(values, shift, 1)[pick, :columns]

    lane = lax.broadcasted_iota(jnp.int32, (8, LANES), 1)
    for at in range(1, len(levels)):
        inner = 1 << at
        group = max(inner, 8)
        source, target = pair_refs[(at + 1) % 2], pair_refs[at % 2]
        last = at == len(levels) - 1
        for block in range(index_ref.shape[1] // LANES if last else blocks):
            lanes = slice(block * LANES, (block + 1) * LANES)
            ahead = min(block + 1, blocks - 1)
            beyond_lanes = slice(ahead * LANES, (ahead + 1) * LANES)

            def load(part, where):
                if at == 1:
                    return jnp.broadcast_to(
                        jnp.concatenate([rows_ref[part, 0:2, where]] * 4, axis=0), (8, LANES)
                    )
                return source[part, :group, where]

            for side in range(2):
                row = 2 * at + side
                step = jnp.broadcast_to(rows_ref[0, row : row + 1, lanes], (8, LANES))
                cos_out = jnp.broadcast_to(rows_ref[1, row : row + 1, lanes], (8, LANES))
                sin_out = jnp.broadcast_to(rows_ref[2, row : row + 1, lanes], (8, LANES))
                index = lane + step.astype(jnp.int32)
                beyond = index >= LANES
                index = index & (LANES - 1)
                for sub in range(group // 8):
                    cut = slice(8 * sub, 8 * sub + 8)
                    moved, cos_in, sin_in = (
                        picked(
                            load(part, lanes)[cut], load(part, beyond_lanes)[cut], index, beyond
                        )
                        for part in range(3)
                    )
                    real = cos_out * cos_in - sin_out * sin_in
                    imag = cos_out * sin_in + sin_out * cos_in
                    moved = moved + step
                    used = min(inner, 8)
                    rows = slice(side * inner + 8 * sub, side * inner + 8 * sub + used)
                    if last:
                        index_ref[rows, lanes] = (lane + moved.astype(jnp.int32))[:used]
                        trig_ref[0, rows, lanes] = real[:used]
                        trig_ref[1, rows, lanes] = imag[:used]
                    else:
                        target[0, rows, lanes] = moved[:used]
                        target[1, rows, lanes] = real[:used]
                        target[2, rows, lanes] = imag[:used]


def steer_kernel(levels, total, offset_ref, phase_ref, left_ref, right_ref, index_ref, trig_ref, rows_ref, even_ref, odd_ref):
    steer(
        levels,
        total,
        offset_ref,
        phase_ref,
        left_ref,
        right_ref,
        rows_ref,
        (even_ref, odd_ref),
        index_ref,
        trig_ref,
    )


def steer_scratch(count, columns):
    rows = max(8, 1 << (count - 1))
    return [VMEM((3, 2 * count, columns), F32)] + [VMEM((3, rows, columns), F32)] * 2


def combination(index_ref, trig_ref, row, lanes, rows):
    def spread(values):
        return jnp.broadcast_to(values, (rows, LANES))

    index = spread(index_ref[row : row + 1, lanes])
    cosine = spread(trig_ref[0, row : row + 1, lanes])
    sine = spread(trig_ref[1, row : row + 1, lanes])
    return index & (LANES - 1), index >= LANES, cosine, sine


def term_of(here, following, steering):
    index, beyond, cosine, sine = steering
    real, imag = (picked(a, b, index, beyond) for a, b in zip(here, following))
    return real * cosine - imag * sine, real * sine + imag * cosine


def sums_and_differences(values):
    values = list(values)
    distance = 1
    while distance < len(values):
        for at in range(len(values)):
            if not at & distance:
                low, high = values[at], values[at + distance]
                values[at], values[at + distance] = low + high, low - high
        distance *= 2
    return values


def first_merges_kernel(
    levels,
    total,
    raw_ref,
    left_ref,
    right_ref,
    table_ref,
    offset_ref,
    phase_ref,
    out_ref,
    field_ref,
    term_ref,
    index_ref,
    trig_ref,
    rows_ref,
    even_ref,
    odd_ref,
):
    pulses, width = raw_ref.shape[1], raw_ref.shape[2]
    blocks = out_ref.shape[2] // LANES
    start = lax.axis_index("rg") * width - LEAD
    dims = (((1,), (1,)), ((), ()))
    for block in range(blocks):
        parts = []
        for part in range(2):
            tiles = []
            for tile in (block, block + 1):
                if tile == 0:
                    tiles.append(left_ref[part * pulses : (part + 1) * pulses, :])
                elif tile == blocks:
                    tiles.append(right_ref[part * pulses : (part + 1) * pulses, :])
                else:
                    tiles.append(raw_ref[part, :, (tile - 1) * LANES : tile * LANES])
            parts.append(
                lax.dot_general(
                    jnp.concatenate(tiles, axis=1),
                    table_ref[part],
                    dims,
                    preferred_element_type=F32,
                )
            )
        both = parts[0] + parts[1]
        if block in (0, blocks - 1):
            bins = start + block * LANES + (
                lax.broadcasted_iota(jnp.int32, both.shape, 1) % LANES
            )
            both = jnp.where((bins >= 0) & (bins < total), both, 0.0)
        lanes = slice(block * LANES, (block + 1) * LANES)
        field_ref[0, :, lanes] = both[:, :LANES]
        field_ref[1, :, lanes] = both[:, LANES:]
    steer(
        range(levels),
        total,
        offset_ref,
        phase_ref,
        left_ref,
        right_ref,
        rows_ref,
        (even_ref, odd_ref),
        index_ref,
        trig_ref,
    )
    combinations = 1 << levels
    chunk = pulses // combinations

    def merge_block(block, carry):
        lanes = at_block(block)
        beyond = at_block(jnp.minimum(block + 1, blocks - 1))
        for at in range(combinations):
            steering = combination(index_ref, trig_ref, at, lanes, chunk)
            rows = slice(at * chunk, (at + 1) * chunk)
            here = [field_ref[part, rows, lanes] for part in range(2)]
            following = [field_ref[part, rows, beyond] for part in range(2)]
            term_ref[0, at], term_ref[1, at] = term_of(here, following, steering)
        for tile in range(chunk // 8):
            cut = slice(8 * tile, 8 * tile + 8)
            real, imag = (
                sums_and_differences([term_ref[part, at, cut] for at in range(combinations)])
                for part in range(2)
            )
            for at in range(combinations):
                out_ref[at * (chunk // 8) + tile, :, lanes] = jnp.concatenate(
                    [real[at], imag[at]], axis=0
                ).astype(BF16)
        return carry

    lax.fori_loop(0, blocks, merge_block, 0)


def last_merges_kernel(target_ref, moved_ref, index_ref, trig_ref, out_ref, term_ref):
    holders, _, columns = moved_ref.shape
    per_tile = out_ref.shape[2] // LANES
    out_blocks = out_ref.shape[0] // holders * per_tile
    tiles_across = out_blocks // per_tile

    def merge_block(block, carry):
        lanes = at_block(block)
        beyond = at_block(block + 1)
        for at in range(holders):
            steering = combination(index_ref, trig_ref, at, lanes, 8)
            here = moved_ref[at, :, lanes].astype(F32)
            following = moved_ref[at, :, beyond].astype(F32)
            term_ref[0, at], term_ref[1, at] = term_of(
                (here[:8], here[8:]), (following[:8], following[8:]), steering
            )
        real, imag = (
            sums_and_differences([term_ref[part, at] for at in range(holders)])
            for part in range(2)
        )
        inner = at_block(block % per_tile)
        for at in range(holders):
            to = target_ref[at * tiles_across + block // per_tile]
            out_ref[to, :, inner] = jnp.concatenate([real[at], imag[at]], axis=0).astype(BF16)
        return carry

    lax.fori_loop(0, out_blocks, merge_block, 0)


def place_kernel(source_ref, incoming_ref, out_ref):
    rows = out_ref.shape[1]
    tile_bins = incoming_ref.shape[2]
    across = out_ref.shape[2] // tile_bins
    base = pl.program_id(0) * (rows // 8) * across
    for row in range(rows // 8):
        for column in range(across):
            tile = incoming_ref[source_ref[base + row * across + column]].astype(F32)
            for part in range(2):
                out_ref[
                    part, row * 8 : row * 8 + 8, column * tile_bins : (column + 1) * tile_bins
                ] = tile[8 * part : 8 * part + 8]


def per_device(raw_echoes, chirp, range_offsets, phases, tile_table):
    ap_count, rg_count = lax.axis_size("ap"), lax.axis_size("rg")
    devices = ap_count * rg_count
    _, pulses, width = raw_echoes.shape
    level_count = range_offsets.shape[0]
    total = width * rg_count
    outer_levels = ap_count.bit_length() - 1
    inner_levels = level_count - outer_levels
    columns = width + LANES
    tile_rows = pulses // ap_count
    tile_bins = width // rg_count
    rim_rows = 2 * pulses + 8 * level_count
    shape = jax.ShapeDtypeStruct

    edge = (2, pulses, LANES)
    last_edge = width // LANES - 1
    to_left, to_right = pl.pallas_call(
        rim_kernel,
        grid=(1,),
        out_shape=[VMEM((rim_rows, LANES), BF16)] * 2,
        compiler_params=params(),
        in_specs=[
            pl.BlockSpec(edge, lambda i: (0, 0, 0)),
            pl.BlockSpec(edge, lambda i: (0, 0, last_edge)),
        ]
        + whole(2),
        out_specs=whole(2),
    )(raw_echoes, raw_echoes, *map(near, (range_offsets, phases)))
    ends = rg_count - 1
    from_left = lax.ppermute(to_right, "rg", [(i, i + 1) for i in range(ends)])
    from_right = lax.ppermute(to_left, "rg", [(i + 1, i) for i in range(ends)])
    table = pl.pallas_call(
        toeplitz_kernel,
        out_shape=VMEM((2, 2 * LANES, 2 * LANES), BF16),
        compiler_params=params(),
        in_specs=whole(1),
        out_specs=whole(1)[0],
    )(chirp)
    inner = 1 << inner_levels
    merged = pl.pallas_call(
        functools.partial(first_merges_kernel, inner_levels, total),
        out_shape=VMEM((ap_count, 2 * tile_rows, columns), BF16),
        compiler_params=params(),
        in_specs=whole(6),
        out_specs=whole(1)[0],
        scratch_shapes=[
            VMEM((2, pulses, columns), F32),
            VMEM((2, inner, pulses // inner, LANES), F32),
            VMEM((inner, columns), jnp.int32),
            VMEM((2, inner, columns), F32),
        ]
        + steer_scratch(inner_levels, columns),
    )(*map(near, (raw_echoes, from_left, from_right, table, range_offsets, phases)))
    moved = lax.all_to_all(merged, "ap", split_axis=0, concat_axis=0, tiled=True)
    index, trig = pl.pallas_call(
        functools.partial(steer_kernel, range(inner_levels, level_count), total),
        out_shape=[VMEM((ap_count, width), jnp.int32), VMEM((2, ap_count, width), F32)],
        compiler_params=params(),
        in_specs=whole(4),
        out_specs=whole(2),
        scratch_shapes=steer_scratch(outer_levels, columns),
    )(*map(near, (range_offsets, phases, from_left, from_right)))

    ap_here, rg_here = lax.axis_index("ap"), lax.axis_index("rg")
    slot_row = tile_table // (rg_count * rg_count)
    slot_col = tile_table % (rg_count * rg_count)
    target = slot_row // ap_count * rg_count + slot_col // rg_count
    shaped = (ap_count, ap_count, rg_count, rg_count)
    target = target.reshape(shaped)
    local_slot = (slot_row % ap_count * rg_count + slot_col % rg_count).reshape(shaped)
    mine = target == ap_here * rg_count + rg_here
    slot_from = jnp.sum(jnp.where(mine, local_slot, 0), axis=(0, 3)).reshape(devices)
    ids = jnp.arange(devices, dtype=jnp.int32)
    source = jnp.sum(
        jnp.where(slot_from[None, :] == ids[:, None], ids[None, :], 0), axis=1
    )
    send_to = lax.dynamic_slice(
        target, (0, ap_here, rg_here, 0), (ap_count, 1, 1, rg_count)
    ).reshape(devices)

    outgoing = pl.pallas_call(
        last_merges_kernel,
        out_shape=VMEM((devices, 2 * tile_rows, tile_bins), BF16),
        compiler_params=params(),
        grid_spec=pltpu.PrefetchScalarGridSpec(
            num_scalar_prefetch=1,
            in_specs=whole(3),
            out_specs=whole(1)[0],
            scratch_shapes=[VMEM((2, ap_count, tile_rows, LANES), F32)],
        ),
    )(send_to, *map(near, (moved, index, trig)))
    incoming = lax.all_to_all(outgoing, ("ap", "rg"), split_axis=0, concat_axis=0, tiled=True)
    steps = 8
    return pl.pallas_call(
        place_kernel,
        out_shape=shape((2, pulses, width), F32),
        compiler_params=params(),
        grid_spec=pltpu.PrefetchScalarGridSpec(
            num_scalar_prefetch=1,
            grid=(steps,),
            in_specs=whole(1),
            out_specs=pl.BlockSpec((2, pulses // steps, width), lambda i, s: (0, i, 0)),
        ),
    )(source, near(incoming))


def solution(mesh):
    placed = (P(None, "ap", "rg"), P(), P(None, None, "rg"), P(None, None, "rg"), P())
    return jax.shard_map(
        per_device, mesh=mesh, in_specs=placed, out_specs=P(None, "ap", "rg"), check_vma=False
    )
```

```python
import functools
import math

import jax
import jax.numpy as jnp
from jax import lax
from jax.experimental import pallas as pl
from jax.experimental.pallas import tpu as pltpu
from jax.sharding import PartitionSpec as P

ROOT_HALF = 0.7071067811865476
LANES = 128
STEP = 8
LEAD = 64
VMEM = pltpu.VMEM
BF16 = jnp.bfloat16
F32 = jnp.float32


def whole(count):
    return [pl.BlockSpec(memory_space=VMEM)] * count


def near(value):
    return pltpu.with_memory_space_constraint(value, VMEM)


def far(value):
    return pltpu.with_memory_space_constraint(value, pltpu.HBM)


def params():
    return pltpu.CompilerParams(vmem_limit_bytes=24 * 2**20)


def at_block(block):
    return pl.ds(pl.multiple_of(block * LANES, LANES), LANES)


def split_three(values):
    high = values.astype(BF16)
    rest = values - high.astype(F32)
    middle = rest.astype(BF16)
    low = (rest - middle.astype(F32)).astype(BF16)
    return high, middle, low


def rim_kernel(raw_ref, offset_ref, phase_ref, left_ref, right_ref, offset_rim, phase_rim, semaphore):
    _, pulses, width = raw_ref.shape
    levels = offset_ref.shape[0]
    rows = 2 * levels
    copies = []
    for side, (out_ref, start) in enumerate(((left_ref, 0), (right_ref, width - LANES))):
        cut = pl.ds(start, LANES)
        for source, target in (
            (raw_ref.at[0, :, cut], out_ref.at[:pulses]),
            (raw_ref.at[1, :, cut], out_ref.at[pulses : 2 * pulses]),
            (offset_ref.at[:, :, cut], offset_rim.at[side]),
            (phase_ref.at[:, :, cut], phase_rim.at[side]),
        ):
            copy = pltpu.make_async_copy(source, target, semaphore.at[len(copies)])
            copy.start()
            copies.append(copy)
    for copy in copies:
        copy.wait()
    for side, out_ref in enumerate((left_ref, right_ref)):
        at = 2 * pulses
        offsets = jnp.concatenate([offset_rim[side, l] for l in range(levels)], axis=0)
        angles = jnp.concatenate([phase_rim[side, l] for l in range(levels)], axis=0)
        out_ref[at : at + rows] = offsets.astype(F32).astype(BF16)
        for part in split_three(angles):
            at += rows
            out_ref[at : at + rows] = part


def toeplitz_kernel(chirp_ref, table_ref):
    taps = chirp_ref[...].astype(BF16).astype(F32)
    zeros = jnp.zeros((1, LANES), F32)
    rolled = []
    for part in range(2):
        row = jnp.concatenate([taps[part : part + 1], zeros], axis=1)
        spread = jnp.broadcast_to(row, (LANES, 2 * LANES))
        rolled.append(pltpu.roll(spread, 0, 1, stride=1, stride_axis=0))
    real, imag = rolled
    table_ref[0] = jnp.concatenate([real, -imag], axis=0).astype(BF16)
    table_ref[1] = jnp.concatenate([imag, real], axis=0).astype(BF16)


def gathered(values, index):
    return jnp.take_along_axis(values, index, axis=1, mode="promise_in_bounds")


def picked(here, following, index, beyond):
    return jnp.where(beyond, gathered(following, index), gathered(here, index))


def steer(
    levels,
    total,
    inner_blocks,
    out_blocks,
    offset_ref,
    phase_ref,
    rims,
    rows_ref,
    pair_refs,
    index_ref,
    trig_ref,
):
    all_levels, _, width = offset_ref.shape
    columns = rows_ref.shape[2]
    blocks = columns // LANES
    rim_rows = 2 * all_levels
    first, count = levels[0], 2 * len(levels)
    start = lax.axis_index("rg") * width - LANES

    def rim(ref):
        if ref is None:
            blank = jnp.zeros((count, LANES), F32)
            return blank, blank
        base = ref.shape[0] - 4 * rim_rows
        aligned = first * 2 // 16 * 16
        parts = [
            ref[base + k * rim_rows + aligned : base + (k + 1) * rim_rows, :].astype(F32)[
                2 * first - aligned : 2 * first - aligned + count
            ]
            for k in range(4)
        ]
        return parts[0], parts[1] + parts[2] + parts[3]

    (left_offset, left_phase), (right_offset, right_phase) = map(rim, rims)
    middle_offset = jnp.concatenate([offset_ref[l] for l in levels], axis=0).astype(F32)
    middle_phase = jnp.concatenate([phase_ref[l] for l in levels], axis=0)
    offsets = jnp.concatenate([left_offset, middle_offset, right_offset], axis=1)
    angles = jnp.concatenate([left_phase, middle_phase, right_phase], axis=1)
    padded = width + 2 * LANES
    bins = start + lax.broadcasted_iota(jnp.int32, (count, padded), 1)
    inside = (bins >= 0) & (bins < total)
    cosine = jnp.where(inside, jnp.cos(angles) * ROOT_HALF, 0.0)
    sine = jnp.where(inside, jnp.sin(angles) * ROOT_HALF, 0.0)
    for at, level in enumerate(levels):
        shift = padded - (LANES - LEAD + STEP * (level + 1))
        pick = slice(2 * at, 2 * at + 2)
        for part, values in enumerate((offsets + (STEP - 4.0), cosine, sine)):
            rows_ref[part, pick] = pltpu.roll(values, shift, 1)[pick, :columns]

    lane = lax.broadcasted_iota(jnp.int32, (8, LANES), 1)
    for at in range(1, len(levels)):
        inner = 1 << at
        group = max(inner, 8)
        source, target = pair_refs[(at + 1) % 2], pair_refs[at % 2]
        last = at == len(levels) - 1
        for block in out_blocks if last else inner_blocks:
            lanes = slice(block * LANES, (block + 1) * LANES)
            ahead = min(block + 1, blocks - 1)
            beyond_lanes = slice(ahead * LANES, (ahead + 1) * LANES)

            def load(part, where):
                if at == 1:
                    return jnp.broadcast_to(
                        jnp.concatenate([rows_ref[part, 0:2, where]] * 4, axis=0), (8, LANES)
                    )
                return source[part, :group, where]

            for side in range(2):
                row = 2 * at + side
                step = jnp.broadcast_to(rows_ref[0, row : row + 1, lanes], (8, LANES))
                cos_out = jnp.broadcast_to(rows_ref[1, row : row + 1, lanes], (8, LANES))
                sin_out = jnp.broadcast_to(rows_ref[2, row : row + 1, lanes], (8, LANES))
                index = lane + step.astype(jnp.int32)
                beyond = index >= LANES
                index = index & (LANES - 1)
                for sub in range(group // 8):
                    cut = slice(8 * sub, 8 * sub + 8)
                    moved, cos_in, sin_in = (
                        picked(
                            load(part, lanes)[cut], load(part, beyond_lanes)[cut], index, beyond
                        )
                        for part in range(3)
                    )
                    real = cos_out * cos_in - sin_out * sin_in
                    imag = cos_out * sin_in + sin_out * cos_in
                    moved = moved + step
                    used = min(inner, 8)
                    rows = slice(side * inner + 8 * sub, side * inner + 8 * sub + used)
                    if last:
                        index_ref[rows, lanes] = (lane + moved.astype(jnp.int32))[:used]
                        trig_ref[0, rows, lanes] = real[:used]
                        trig_ref[1, rows, lanes] = imag[:used]
                    else:
                        target[0, rows, lanes] = moved[:used]
                        target[1, rows, lanes] = real[:used]
                        target[2, rows, lanes] = imag[:used]


def steer_kernel(
    levels,
    total,
    offset_ref,
    phase_ref,
    left_ref,
    right_ref,
    index_ref,
    trig_ref,
    rows_ref,
    even_ref,
    odd_ref,
):
    steer(
        levels,
        total,
        range(rows_ref.shape[2] // LANES),
        range(index_ref.shape[1] // LANES),
        offset_ref,
        phase_ref,
        (left_ref, right_ref),
        rows_ref,
        (even_ref, odd_ref),
        index_ref,
        trig_ref,
    )


def steer_scratch(count, columns):
    rows = max(8, 1 << (count - 1))
    return [VMEM((3, 2 * count, columns), F32)] + [VMEM((3, rows, columns), F32)] * 2


def combination(index_ref, trig_ref, row, lanes, rows):
    def spread(values):
        return jnp.broadcast_to(values, (rows, LANES))

    index = spread(index_ref[row : row + 1, lanes])
    cosine = spread(trig_ref[0, row : row + 1, lanes])
    sine = spread(trig_ref[1, row : row + 1, lanes])
    return index & (LANES - 1), index >= LANES, cosine, sine


def term_of(here, following, steering):
    index, beyond, cosine, sine = steering
    real, imag = (picked(a, b, index, beyond) for a, b in zip(here, following))
    return real * cosine - imag * sine, real * sine + imag * cosine


def sums_and_differences(values):
    values = list(values)
    distance = 1
    while distance < len(values):
        for at in range(len(values)):
            if not at & distance:
                low, high = values[at], values[at + distance]
                values[at], values[at + distance] = low + high, low - high
        distance *= 2
    return values


def filter_block(tiles, table_ref):
    parts = [
        lax.dot_general(
            jnp.concatenate(tiles[part], axis=1),
            table_ref[part],
            (((1,), (1,)), ((), ())),
            preferred_element_type=F32,
        )
        for part in range(2)
    ]
    return parts[0] + parts[1]


def merge_first(levels, field_ref, here_lanes, next_lanes, lanes, index_ref, trig_ref, term_ref, out_ref):
    pulses = field_ref.shape[1]
    combinations = 1 << levels
    chunk = pulses // combinations
    for at in range(combinations):
        steering = combination(index_ref, trig_ref, at, lanes, chunk)
        rows = slice(at * chunk, (at + 1) * chunk)
        here = [field_ref[part, rows, here_lanes] for part in range(2)]
        following = [field_ref[part, rows, next_lanes] for part in range(2)]
        term_ref[0, at], term_ref[1, at] = term_of(here, following, steering)
    for tile in range(chunk // 8):
        cut = slice(8 * tile, 8 * tile + 8)
        real, imag = (
            sums_and_differences([term_ref[part, at, cut] for at in range(combinations)])
            for part in range(2)
        )
        for at in range(combinations):
            out_ref[at * (chunk // 8) + tile, :, lanes] = jnp.concatenate(
                [real[at], imag[at]], axis=0
            ).astype(BF16)


def inner_merges_kernel(
    levels,
    total,
    raw_ref,
    table_ref,
    offset_ref,
    phase_ref,
    out_ref,
    ends_ref,
    field_ref,
    term_ref,
    index_ref,
    trig_ref,
    rows_ref,
    even_ref,
    odd_ref,
):
    tiles = raw_ref.shape[2] // LANES
    for block in range(1, tiles):
        cut = slice((block - 1) * LANES, (block + 1) * LANES)
        both = filter_block([[raw_ref[part, :, cut]] for part in range(2)], table_ref)
        lanes = slice(block * LANES, (block + 1) * LANES)
        for part in range(2):
            values = both[:, part * LANES : (part + 1) * LANES]
            field_ref[part, :, lanes] = values
            if block == 1:
                ends_ref[part, :, :LANES] = values
            if block == tiles - 1:
                ends_ref[part, :, LANES:] = values
    steer(
        range(levels),
        total,
        range(1, tiles),
        range(1, tiles - 1),
        offset_ref,
        phase_ref,
        (None, None),
        rows_ref,
        (even_ref, odd_ref),
        index_ref,
        trig_ref,
    )

    def merge_block(block, carry):
        lanes, beyond = at_block(block), at_block(block + 1)
        merge_first(
            levels, field_ref, lanes, beyond, lanes, index_ref, trig_ref, term_ref, out_ref
        )
        return carry

    lax.fori_loop(1, tiles - 1, merge_block, 0)


def outer_merges_kernel(
    levels,
    total,
    partial_ref,
    ends_ref,
    raw_ref,
    left_ref,
    right_ref,
    table_ref,
    offset_ref,
    phase_ref,
    out_ref,
    field_ref,
    term_ref,
    index_ref,
    trig_ref,
    rows_ref,
    even_ref,
    odd_ref,
):
    pulses, width = raw_ref.shape[1], raw_ref.shape[2]
    tiles = width // LANES
    start = lax.axis_index("rg") * width - LEAD

    def held(position):
        return slice(position * LANES, (position + 1) * LANES)

    for position, block in ((0, 0), (3, tiles)):
        pair = []
        for part in range(2):
            rows = slice(part * pulses, (part + 1) * pulses)
            if block == 0:
                pair.append([left_ref[rows, :], raw_ref[part, :, :LANES]])
            else:
                pair.append([raw_ref[part, :, width - LANES :], right_ref[rows, :]])
        both = filter_block(pair, table_ref)
        bins = start + block * LANES + (lax.broadcasted_iota(jnp.int32, both.shape, 1) % LANES)
        both = jnp.where((bins >= 0) & (bins < total), both, 0.0)
        for part in range(2):
            field_ref[part, :, held(position)] = both[:, part * LANES : (part + 1) * LANES]
    for part in range(2):
        field_ref[part, :, LANES : 3 * LANES] = ends_ref[part]
    middle = slice(LANES, (tiles - 1) * LANES)
    out_ref[:, :, middle] = partial_ref[:, :, middle]
    steer(
        range(levels),
        total,
        (0, 1, tiles - 1, tiles),
        (0, tiles - 1, tiles),
        offset_ref,
        phase_ref,
        (left_ref, right_ref),
        rows_ref,
        (even_ref, odd_ref),
        index_ref,
        trig_ref,
    )
    for here, following, block in ((0, 1, 0), (2, 3, tiles - 1), (3, 3, tiles)):
        merge_first(
            levels,
            field_ref,
            held(here),
            held(following),
            slice(block * LANES, (block + 1) * LANES),
            index_ref,
            trig_ref,
            term_ref,
            out_ref,
        )


def last_merges_kernel(target_ref, moved_ref, index_ref, trig_ref, out_ref, term_ref):
    holders, _, columns = moved_ref.shape
    per_tile = out_ref.shape[2] // LANES
    out_blocks = out_ref.shape[0] // holders * per_tile
    tiles_across = out_blocks // per_tile

    def merge_block(block, carry):
        lanes = at_block(block)
        beyond = at_block(block + 1)
        for at in range(holders):
            steering = combination(index_ref, trig_ref, at, lanes, 8)
            here = moved_ref[at, :, lanes].astype(F32)
            following = moved_ref[at, :, beyond].astype(F32)
            term_ref[0, at], term_ref[1, at] = term_of(
                (here[:8], here[8:]), (following[:8], following[8:]), steering
            )
        real, imag = (
            sums_and_differences([term_ref[part, at] for at in range(holders)])
            for part in range(2)
        )
        inner = at_block(block % per_tile)
        for at in range(holders):
            to = target_ref[at * tiles_across + block // per_tile]
            out_ref[to, :, inner] = jnp.concatenate([real[at], imag[at]], axis=0).astype(BF16)
        return carry

    lax.fori_loop(0, out_blocks, merge_block, 0)


def place_kernel(steps, source_ref, incoming_ref, out_ref, image_ref, semaphore):
    _, rows, width = out_ref.shape
    tile_bins = incoming_ref.shape[2]
    across = width // tile_bins
    share = rows // steps
    copies = []
    for step in range(steps):
        for row in range(step * share // 8, (step + 1) * share // 8):
            for column in range(across):
                tile = incoming_ref[source_ref[row * across + column]].astype(F32)
                for part in range(2):
                    image_ref[
                        part, row * 8 : row * 8 + 8, column * tile_bins : (column + 1) * tile_bins
                    ] = tile[8 * part : 8 * part + 8]
        cut = pl.ds(step * share, share)
        copy = pltpu.make_async_copy(
            image_ref.at[:, cut, :], out_ref.at[:, cut, :], semaphore.at[step]
        )
        copy.start()
        copies.append(copy)
    for copy in copies:
        copy.wait()


def per_device(raw_echoes, chirp, range_offsets, phases, tile_table):
    ap_count, rg_count = lax.axis_size("ap"), lax.axis_size("rg")
    devices = ap_count * rg_count
    _, pulses, width = raw_echoes.shape
    level_count = range_offsets.shape[0]
    total = width * rg_count
    outer_levels = ap_count.bit_length() - 1
    inner_levels = level_count - outer_levels
    columns = width + LANES
    tile_rows = pulses // ap_count
    tile_bins = width // rg_count
    rim_rows = 2 * pulses + 8 * level_count
    shape = jax.ShapeDtypeStruct

    anywhere = pl.BlockSpec(memory_space=pl.ANY)
    to_left, to_right = pl.pallas_call(
        rim_kernel,
        out_shape=[VMEM((rim_rows, LANES), BF16)] * 2,
        compiler_params=params(),
        in_specs=[pl.BlockSpec(memory_space=pltpu.HBM)] * 3,
        out_specs=whole(2),
        scratch_shapes=[
            VMEM((2, level_count, 2, LANES), jnp.int32),
            VMEM((2, level_count, 2, LANES), F32),
            pltpu.SemaphoreType.DMA((8,)),
        ],
    )(*map(far, (raw_echoes, range_offsets, phases)))
    ends = rg_count - 1
    from_left = lax.ppermute(to_right, "rg", [(i, i + 1) for i in range(ends)])
    from_right = lax.ppermute(to_left, "rg", [(i + 1, i) for i in range(ends)])
    table = pl.pallas_call(
        toeplitz_kernel,
        out_shape=VMEM((2, 2 * LANES, 2 * LANES), BF16),
        compiler_params=params(),
        in_specs=whole(1),
        out_specs=whole(1)[0],
    )(chirp)
    inner = 1 << inner_levels
    near_raw, near_offsets, near_phases = map(near, (raw_echoes, range_offsets, phases))
    merged_shape = VMEM((ap_count, 2 * tile_rows, columns), BF16)

    def first_scratch(held):
        return [
            VMEM((2, pulses, held), F32),
            VMEM((2, inner, pulses // inner, LANES), F32),
            VMEM((inner, columns), jnp.int32),
            VMEM((2, inner, columns), F32),
        ] + steer_scratch(inner_levels, columns)

    partial, field_ends = pl.pallas_call(
        functools.partial(inner_merges_kernel, inner_levels, total),
        out_shape=[merged_shape, VMEM((2, pulses, 2 * LANES), F32)],
        compiler_params=params(),
        in_specs=whole(4),
        out_specs=whole(2),
        scratch_shapes=first_scratch(columns),
    )(near_raw, near(table), near_offsets, near_phases)
    merged = pl.pallas_call(
        functools.partial(outer_merges_kernel, inner_levels, total),
        out_shape=merged_shape,
        compiler_params=params(),
        in_specs=whole(8),
        out_specs=whole(1)[0],
        scratch_shapes=first_scratch(4 * LANES),
    )(
        *map(near, (partial, field_ends)),
        near_raw,
        *map(near, (from_left, from_right, table)),
        near_offsets,
        near_phases,
    )
    moved = lax.all_to_all(merged, "ap", split_axis=0, concat_axis=0, tiled=True)
    index, trig = pl.pallas_call(
        functools.partial(steer_kernel, range(inner_levels, level_count), total),
        out_shape=[VMEM((ap_count, width), jnp.int32), VMEM((2, ap_count, width), F32)],
        compiler_params=params(),
        in_specs=whole(4),
        out_specs=whole(2),
        scratch_shapes=steer_scratch(outer_levels, columns),
    )(near_offsets, near_phases, *map(near, (from_left, from_right)))

    ap_here, rg_here = lax.axis_index("ap"), lax.axis_index("rg")
    slot_row = tile_table // (rg_count * rg_count)
    slot_col = tile_table % (rg_count * rg_count)
    target = slot_row // ap_count * rg_count + slot_col // rg_count
    shaped = (ap_count, ap_count, rg_count, rg_count)
    target = target.reshape(shaped)
    local_slot = (slot_row % ap_count * rg_count + slot_col % rg_count).reshape(shaped)
    mine = target == ap_here * rg_count + rg_here
    slot_from = jnp.sum(jnp.where(mine, local_slot, 0), axis=(0, 3)).reshape(devices)
    ids = jnp.arange(devices, dtype=jnp.int32)
    source = jnp.sum(
        jnp.where(slot_from[None, :] == ids[:, None], ids[None, :], 0), axis=1
    )
    send_to = lax.dynamic_slice(
        target, (0, ap_here, rg_here, 0), (ap_count, 1, 1, rg_count)
    ).reshape(devices)

    outgoing = pl.pallas_call(
        last_merges_kernel,
        out_shape=VMEM((devices, 2 * tile_rows, tile_bins), BF16),
        compiler_params=params(),
        grid_spec=pltpu.PrefetchScalarGridSpec(
            num_scalar_prefetch=1,
            in_specs=whole(3),
            out_specs=whole(1)[0],
            scratch_shapes=[VMEM((2, ap_count, tile_rows, LANES), F32)],
        ),
    )(send_to, *map(near, (moved, index, trig)))
    incoming = lax.all_to_all(outgoing, ("ap", "rg"), split_axis=0, concat_axis=0, tiled=True)
    steps = 4
    return pl.pallas_call(
        functools.partial(place_kernel, steps),
        out_shape=shape((2, pulses, width), F32),
        compiler_params=params(),
        grid_spec=pltpu.PrefetchScalarGridSpec(
            num_scalar_prefetch=1,
            in_specs=whole(1),
            out_specs=anywhere,
            scratch_shapes=[VMEM((2, pulses, width), F32), pltpu.SemaphoreType.DMA((steps,))],
        ),
    )(source, near(incoming))


def solution(mesh):
    placed = (P(None, "ap", "rg"), P(), P(None, None, "rg"), P(None, None, "rg"), P())
    return jax.shard_map(
        per_device, mesh=mesh, in_specs=placed, out_specs=P(None, "ap", "rg"), check_vma=False
    )
```

```python
import functools
import math

import jax
import jax.numpy as jnp
from jax import lax
from jax.experimental import pallas as pl
from jax.experimental.pallas import tpu as pltpu
from jax.sharding import PartitionSpec as P

ROOT_HALF = 0.7071067811865476
LANES = 128
STEP = 8
LEAD = 64
VMEM = pltpu.VMEM
BF16 = jnp.bfloat16
F32 = jnp.float32


def whole(count):
    return [pl.BlockSpec(memory_space=VMEM)] * count


def near(value):
    return pltpu.with_memory_space_constraint(value, VMEM)


def far(value):
    return pltpu.with_memory_space_constraint(value, pltpu.HBM)


def params():
    return pltpu.CompilerParams(vmem_limit_bytes=24 * 2**20)


def at_block(block):
    return pl.ds(pl.multiple_of(block * LANES, LANES), LANES)


def split_three(values):
    high = values.astype(BF16)
    rest = values - high.astype(F32)
    middle = rest.astype(BF16)
    low = (rest - middle.astype(F32)).astype(BF16)
    return high, middle, low


def rim_kernel(
    raw_ref,
    chirp_ref,
    offset_ref,
    phase_ref,
    left_ref,
    right_ref,
    near_chirp,
    near_offset,
    near_phase,
    semaphore,
):
    _, pulses, width = raw_ref.shape
    levels = offset_ref.shape[0]
    rows = 2 * levels
    copies = []
    for source, target in (
        (offset_ref, near_offset),
        (phase_ref, near_phase),
        (raw_ref.at[0, :, pl.ds(0, LANES)], left_ref.at[:pulses]),
        (raw_ref.at[1, :, pl.ds(0, LANES)], left_ref.at[pulses : 2 * pulses]),
        (raw_ref.at[0, :, pl.ds(width - LANES, LANES)], right_ref.at[:pulses]),
        (raw_ref.at[1, :, pl.ds(width - LANES, LANES)], right_ref.at[pulses : 2 * pulses]),
        (chirp_ref, near_chirp),
    ):
        copy = pltpu.make_async_copy(source, target, semaphore.at[len(copies)])
        copy.start()
        copies.append(copy)
    for copy in copies[:2]:
        copy.wait()
    for start, out_ref in ((0, left_ref), (width - LANES, right_ref)):
        cut = slice(start, start + LANES)
        at = 2 * pulses
        offsets = jnp.concatenate([near_offset[l, :, cut] for l in range(levels)], axis=0)
        angles = jnp.concatenate([near_phase[l, :, cut] for l in range(levels)], axis=0)
        out_ref[at : at + rows] = offsets.astype(F32).astype(BF16)
        for part in split_three(angles):
            at += rows
            out_ref[at : at + rows] = part
    for copy in copies[2:]:
        copy.wait()


def fill_toeplitz(chirp_ref, table_ref):
    taps = chirp_ref[...].astype(BF16).astype(F32)
    zeros = jnp.zeros((1, LANES), F32)
    rolled = []
    for part in range(2):
        row = jnp.concatenate([taps[part : part + 1], zeros], axis=1)
        spread = jnp.broadcast_to(row, (LANES, 2 * LANES))
        rolled.append(pltpu.roll(spread, 0, 1, stride=1, stride_axis=0))
    real, imag = rolled
    table_ref[0] = jnp.concatenate([real, -imag], axis=0).astype(BF16)
    table_ref[1] = jnp.concatenate([imag, real], axis=0).astype(BF16)


def gathered(values, index):
    return lax.gather(
        values,
        index[:, :, None],
        lax.GatherDimensionNumbers(
            offset_dims=(),
            collapsed_slice_dims=(1,),
            start_index_map=(1,),
            operand_batching_dims=(0,),
            start_indices_batching_dims=(0,),
        ),
        slice_sizes=(1, 1),
        mode=lax.GatherScatterMode.PROMISE_IN_BOUNDS,
    )


def picked(here, following, index, beyond):
    return jnp.where(beyond, gathered(following, index), gathered(here, index))


def scaled_trig(angles):
    return jnp.cos(angles) * ROOT_HALF, jnp.sin(angles) * ROOT_HALF


def align(values, blocks, sources_of, rows_ref):
    width = values[0].shape[1]
    lanes = slice(blocks[0] * LANES, (blocks[-1] + 1) * LANES)
    count = len(blocks) * LANES
    for level, (slot, side) in enumerate(sources_of):
        shift = (width - (LANES - LEAD + STEP * (level + 1))) % width
        group, row = 2 * level // 8 * 8, 2 * level % 8
        for part in range(3):
            moved = values[part][group : group + 8]
            if shift:
                moved = pltpu.roll(moved, shift, 1)
            pair = moved[row : row + 2, :count]
            if side is None:
                rows_ref[part, slot : slot + 2, lanes] = pair
            else:
                rows_ref[part, slot : slot + 1, lanes] = jnp.where(side == 1, pair[1:2], pair[0:1])


def sources(levels, inner_levels):
    here = lax.axis_index("ap")
    return [
        (2 * level, None)
        if level < inner_levels
        else (inner_levels + level, (here >> (level - inner_levels)) & 1)
        for level in range(levels)
    ]


def compose(outer, inner, inner_beyond, lane):
    step, cos_out, sin_out = outer
    index = lane + step.astype(jnp.int32)
    beyond = index >= LANES
    index = index & (LANES - 1)
    moved, cos_in, sin_in = (
        picked(a, b, index, beyond) for a, b in zip(inner, inner_beyond)
    )
    return (
        step + moved,
        cos_out * cos_in - sin_out * sin_in,
        cos_out * sin_in + sin_out * cos_in,
    )


def steer(levels, inner_levels, blocks, rows_ref, index_ref, trig_ref):
    lane = lax.broadcasted_iota(jnp.int32, (8, LANES), 1)
    last = blocks[-1]

    def row(slot, block):
        lanes = slice(block * LANES, (block + 1) * LANES)
        return tuple(
            jnp.broadcast_to(rows_ref[part, slot : slot + 1, lanes], (8, LANES))
            for part in range(3)
        )

    def chain(outer_of, inner):
        return {
            block: compose(outer_of(block), inner[block], inner[min(block + 1, last)], lane)
            for block in blocks
        }

    own = {block: row(2 * inner_levels, block) for block in blocks}
    for level in range(inner_levels + 1, levels):
        own = chain(lambda block: row(inner_levels + level, block), own)

    sublane = lax.broadcasted_iota(jnp.int32, (8, LANES), 0)
    inner = {}
    for block in blocks:
        low, high = row(0, block), row(1, block)
        inner[block] = tuple(
            jnp.where(sublane % 2 == 0, a, b) for a, b in zip(low, high)
        )
    for level in range(1, inner_levels):
        bit = (sublane >> level) & 1

        def outer_of(block):
            low, high = row(2 * level, block), row(2 * level + 1, block)
            return tuple(jnp.where(bit == 0, a, b) for a, b in zip(low, high))

        inner = chain(outer_of, inner)

    for block in blocks[:-1]:
        moved, cosine, sine = compose(own[block], inner[block], inner[block + 1], lane)
        reach = lane + moved.astype(jnp.int32)
        lanes = slice(block * LANES, (block + 1) * LANES)
        index_ref[0, :, lanes] = reach & (LANES - 1)
        index_ref[1, :, lanes] = reach - LANES
        trig_ref[0, :, lanes] = cosine
        trig_ref[1, :, lanes] = sine


def combination(index_ref, trig_ref, row, lanes, rows):
    def spread(values):
        return jnp.broadcast_to(values, (rows, LANES))

    index = spread(index_ref[0, row : row + 1, lanes])
    beyond = spread(index_ref[1, row : row + 1, lanes]) >= 0
    cosine = spread(trig_ref[0, row : row + 1, lanes])
    sine = spread(trig_ref[1, row : row + 1, lanes])
    return index, beyond, cosine, sine


def term_of(here, following, steering):
    index, beyond, cosine, sine = steering
    real, imag = (picked(a, b, index, beyond) for a, b in zip(here, following))
    return real * cosine - imag * sine, real * sine + imag * cosine


def sums_and_differences(values):
    values = list(values)
    distance = 1
    while distance < len(values):
        for at in range(len(values)):
            if not at & distance:
                low, high = values[at], values[at + distance]
                values[at], values[at + distance] = low + high, low - high
        distance *= 2
    return values


def filter_block(tiles, table_ref):
    parts = [
        lax.dot_general(
            jnp.concatenate(tiles[part], axis=1),
            table_ref[part],
            (((1,), (1,)), ((), ())),
            preferred_element_type=F32,
        )
        for part in range(2)
    ]
    return parts[0] + parts[1]


def merge_first(
    levels,
    field_ref,
    here_lanes,
    next_lanes,
    lanes,
    index_ref,
    trig_ref,
    term_ref,
    out_ref,
    out_lanes,
):
    pulses = field_ref.shape[1]
    combinations = 1 << levels
    chunk = pulses // combinations
    for at in range(combinations):
        steering = combination(index_ref, trig_ref, at, lanes, chunk)
        rows = slice(at * chunk, (at + 1) * chunk)
        here = [field_ref[part, rows, here_lanes] for part in range(2)]
        following = [field_ref[part, rows, next_lanes] for part in range(2)]
        term_ref[0, at], term_ref[1, at] = term_of(here, following, steering)
    for tile in range(chunk // 8):
        cut = slice(8 * tile, 8 * tile + 8)
        real, imag = (
            sums_and_differences([term_ref[part, at, cut] for at in range(combinations)])
            for part in range(2)
        )
        for at in range(combinations):
            out_ref[at * (chunk // 8) + tile, :, out_lanes] = jnp.concatenate(
                [real[at], imag[at]], axis=0
            ).astype(BF16)


def inner_merges_kernel(
    inner_levels,
    far_raw,
    chirp_ref,
    offset_ref,
    phase_ref,
    out_ref,
    ends_ref,
    steering_ref,
    table_ref,
    raw_ref,
    loaded,
    stored,
    merged_ref,
    field_ref,
    term_ref,
    index_ref,
    trig_ref,
    rows_ref,
):
    tiles = raw_ref.shape[2] // LANES
    levels = offset_ref.shape[0]
    loading = pltpu.make_async_copy(far_raw, raw_ref, loaded.at[0])
    loading.start()
    offsets = jnp.concatenate([offset_ref[l] for l in range(levels)], axis=0)
    angles = jnp.concatenate([phase_ref[l] for l in range(levels)], axis=0)
    values = (offsets.astype(F32) + (STEP - 4.0), *scaled_trig(angles))
    for part in range(3):
        steering_ref[part] = values[part]
    blank = jnp.zeros((2 * levels, LANES), F32)
    align(
        [jnp.concatenate([blank, value, blank], axis=1) for value in values],
        range(tiles + 1),
        sources(levels, inner_levels),
        rows_ref,
    )
    steer(levels, inner_levels, range(1, tiles), rows_ref, index_ref, trig_ref)
    fill_toeplitz(chirp_ref, table_ref)
    loading.wait()
    for block in range(1, tiles):
        cut = slice((block - 1) * LANES, (block + 1) * LANES)
        both = filter_block([[raw_ref[part, :, cut]] for part in range(2)], table_ref)
        lanes = slice(block * LANES, (block + 1) * LANES)
        for part in range(2):
            values = both[:, part * LANES : (part + 1) * LANES]
            field_ref[part, :, lanes] = values
            if block == 1:
                ends_ref[part, :, :LANES] = values
            if block == tiles - 1:
                ends_ref[part, :, LANES:] = values

    def stored_block(lanes):
        return pltpu.make_async_copy(
            merged_ref.at[:, :, lanes], out_ref.at[:, :, lanes], stored.at[0]
        )

    def merge_pair(pair, carry):
        for slot in range(2):
            block = 1 + 2 * pair + slot
            lanes, beyond = at_block(block), at_block(block + 1)
            merge_first(
                inner_levels,
                field_ref,
                lanes,
                beyond,
                lanes,
                index_ref,
                trig_ref,
                term_ref.at[slot],
                merged_ref,
                lanes,
            )
        both = pl.multiple_of((1 + 2 * pair) * LANES, LANES)
        stored_block(pl.ds(both, 2 * LANES)).start()
        return carry

    lax.fori_loop(0, (tiles - 2) // 2, merge_pair, 0)
    stored_block(pl.ds(LANES, (tiles - 2) * LANES)).wait()


def outer_merges_kernel(
    inner_levels,
    total,
    partial_ref,
    ends_ref,
    steering_ref,
    raw_ref,
    left_ref,
    right_ref,
    table_ref,
    out_ref,
    semaphore,
    merged_ref,
    field_ref,
    term_ref,
    index_ref,
    trig_ref,
    rows_ref,
):
    pulses, width = raw_ref.shape[1], raw_ref.shape[2]
    tiles = width // LANES
    rim_rows = steering_ref.shape[1]
    levels = rim_rows // 2
    start = lax.axis_index("rg") * width - LEAD
    own_sources = sources(levels, inner_levels)

    def held(position):
        return slice(position * LANES, (position + 1) * LANES)

    for rim_ref, at, near_lanes, blocks in (
        (left_ref, -LANES, slice(0, 2 * LANES), (0, 1)),
        (right_ref, width, slice(width - 2 * LANES, width), (tiles - 1, tiles)),
    ):
        offsets, high, middle, low = (
            rim_ref[2 * pulses + k * rim_rows : 2 * pulses + (k + 1) * rim_rows, :].astype(F32)
            for k in range(4)
        )
        cosine, sine = scaled_trig(high + middle + low)
        bins = lax.axis_index("rg") * width + at + lax.broadcasted_iota(
            jnp.int32, (rim_rows, LANES), 1
        )
        inside = (bins >= 0) & (bins < total)
        rim = (
            offsets + (STEP - 4.0),
            jnp.where(inside, cosine, 0.0),
            jnp.where(inside, sine, 0.0),
        )
        middle = [steering_ref[part, :, near_lanes] for part in range(3)]
        joined = [
            jnp.concatenate((a, b) if at < 0 else (b, a), axis=1) for a, b in zip(rim, middle)
        ]
        align(joined, blocks, own_sources, rows_ref)
        steer(levels, inner_levels, blocks, rows_ref, index_ref, trig_ref)

    for position, block in ((0, 0), (3, tiles)):
        pair = []
        for part in range(2):
            rows = slice(part * pulses, (part + 1) * pulses)
            if block == 0:
                pair.append([left_ref[rows, :], raw_ref[part, :, :LANES]])
            else:
                pair.append([raw_ref[part, :, width - LANES :], right_ref[rows, :]])
        both = filter_block(pair, table_ref)
        bins = start + block * LANES + (lax.broadcasted_iota(jnp.int32, both.shape, 1) % LANES)
        both = jnp.where((bins >= 0) & (bins < total), both, 0.0)
        for part in range(2):
            field_ref[part, :, held(position)] = both[:, part * LANES : (part + 1) * LANES]
    for part in range(2):
        field_ref[part, :, LANES : 3 * LANES] = ends_ref[part]
    copies = []
    for here, following, block in ((0, 1, 0), (2, 3, tiles - 1)):
        merge_first(
            inner_levels,
            field_ref,
            held(here),
            held(following),
            slice(block * LANES, (block + 1) * LANES),
            index_ref,
            trig_ref,
            term_ref.at[len(copies)],
            merged_ref.at[len(copies)],
            slice(0, LANES),
        )
        copy = pltpu.make_async_copy(
            merged_ref.at[len(copies)],
            out_ref.at[:, :, pl.ds(block * LANES, LANES)],
            semaphore.at[len(copies)],
        )
        copy.start()
        copies.append(copy)
    for copy in copies:
        copy.wait()


def last_sums_kernel(target_ref, moved_ref, out_ref, tile_ref, term_ref, semaphore):
    holders, rows, columns = moved_ref.shape
    per_tile = out_ref.shape[2] // LANES
    tiles_across = columns // out_ref.shape[2]
    near_group = min(8, holders)
    for column in range(tiles_across):
        for part in range(per_tile):
            block = column * per_tile + part
            lanes = slice(block * LANES, (block + 1) * LANES)
            inner = slice(part * LANES, (part + 1) * LANES)
            slot = block % 2
            for first in range(0, holders, near_group):
                sums = sums_and_differences(
                    [moved_ref[first + at, :, lanes].astype(F32) for at in range(near_group)]
                )
                for at in range(near_group):
                    term_ref[slot, first + at] = sums[at]
            for first in range(near_group):
                members = range(first, holders, near_group)
                sums = sums_and_differences([term_ref[slot, at] for at in members])
                for at, value in zip(members, sums):
                    tile_ref[column, at, :, inner] = value.astype(BF16)
        for at in range(holders):
            to = target_ref[at * tiles_across + column]
            pltpu.make_async_copy(
                tile_ref.at[column, at], out_ref.at[to], semaphore.at[column]
            ).start()
    for column in range(tiles_across):
        pltpu.make_async_copy(
            tile_ref.at[column], out_ref.at[pl.ds(0, holders)], semaphore.at[column]
        ).wait()


def place_kernel(steps, source_ref, incoming_ref, out_ref, image_ref, semaphore):
    _, rows, width = out_ref.shape
    tile_bins = incoming_ref.shape[2]
    across = width // tile_bins
    share = rows // steps
    copies = []
    for step in range(steps):
        for row in range(step * share // 8, (step + 1) * share // 8):
            for column in range(across):
                tile = incoming_ref[source_ref[row * across + column]].astype(F32)
                for part in range(2):
                    image_ref[
                        part, row * 8 : row * 8 + 8, column * tile_bins : (column + 1) * tile_bins
                    ] = tile[8 * part : 8 * part + 8]
        cut = pl.ds(step * share, share)
        copy = pltpu.make_async_copy(
            image_ref.at[:, cut, :], out_ref.at[:, cut, :], semaphore.at[step]
        )
        copy.start()
        copies.append(copy)
    for copy in copies:
        copy.wait()


def per_device(raw_echoes, chirp, range_offsets, phases, tile_table):
    ap_count, rg_count = lax.axis_size("ap"), lax.axis_size("rg")
    devices = ap_count * rg_count
    _, pulses, width = raw_echoes.shape
    level_count = range_offsets.shape[0]
    total = width * rg_count
    outer_levels = ap_count.bit_length() - 1
    inner_levels = level_count - outer_levels
    tile_rows = pulses // ap_count
    tile_bins = width // rg_count
    rim_rows = 2 * pulses + 8 * level_count
    shape = jax.ShapeDtypeStruct

    anywhere = pl.BlockSpec(memory_space=pl.ANY)
    distant = pl.BlockSpec(memory_space=pltpu.HBM)
    to_left, to_right, near_chirp, near_offsets, near_phases = pl.pallas_call(
        rim_kernel,
        out_shape=[VMEM((rim_rows, LANES), BF16)] * 2
        + [
            VMEM(chirp.shape, F32),
            VMEM(range_offsets.shape, jnp.int32),
            VMEM(phases.shape, F32),
        ],
        compiler_params=params(),
        in_specs=[distant] * 4,
        out_specs=whole(5),
        scratch_shapes=[pltpu.SemaphoreType.DMA((7,))],
    )(*map(far, (raw_echoes, chirp, range_offsets, phases)))
    ends = rg_count - 1
    from_left = lax.ppermute(to_right, "rg", [(i, i + 1) for i in range(ends)])
    from_right = lax.ppermute(to_left, "rg", [(i + 1, i) for i in range(ends)])
    inner = 1 << inner_levels
    merged_shape = pltpu.HBM((ap_count, 2 * tile_rows, width), BF16)

    def first_scratch(held):
        return [
            VMEM((2, pulses, held), F32),
            VMEM((2, 2, inner, pulses // inner, LANES), F32),
            VMEM((2, inner, width), jnp.int32),
            VMEM((2, inner, width), F32),
            VMEM((3, inner_levels + level_count, width + LANES), F32),
        ]

    partial, field_ends, steering, table, near_raw = pl.pallas_call(
        functools.partial(inner_merges_kernel, inner_levels),
        out_shape=[
            merged_shape,
            VMEM((2, pulses, 2 * LANES), F32),
            VMEM((3, 2 * level_count, width), F32),
            VMEM((2, 2 * LANES, 2 * LANES), BF16),
            VMEM(raw_echoes.shape, BF16),
        ],
        compiler_params=params(),
        in_specs=[distant] + whole(3),
        out_specs=[distant] + whole(4),
        scratch_shapes=[
            pltpu.SemaphoreType.DMA((1,)),
            pltpu.SemaphoreType.DMA((1,)),
            VMEM((ap_count, 2 * tile_rows, width), BF16),
        ]
        + first_scratch(width),
    )(far(raw_echoes), *map(near, (near_chirp, near_offsets, near_phases)))
    merged = pl.pallas_call(
        functools.partial(outer_merges_kernel, inner_levels, total),
        out_shape=merged_shape,
        compiler_params=params(),
        in_specs=[distant] + whole(6),
        out_specs=distant,
        input_output_aliases={0: 0},
        scratch_shapes=[
            pltpu.SemaphoreType.DMA((2,)),
            VMEM((2, ap_count, 2 * tile_rows, LANES), BF16),
        ]
        + first_scratch(4 * LANES),
    )(
        far(partial),
        *map(near, (field_ends, steering, near_raw, from_left, from_right, table)),
    )
    moved = lax.all_to_all(merged, "ap", split_axis=0, concat_axis=0, tiled=True)

    ap_here, rg_here = lax.axis_index("ap"), lax.axis_index("rg")
    slot_row = tile_table // (rg_count * rg_count)
    slot_col = tile_table % (rg_count * rg_count)
    target = slot_row // ap_count * rg_count + slot_col // rg_count
    shaped = (ap_count, ap_count, rg_count, rg_count)
    target = target.reshape(shaped)
    local_slot = (slot_row % ap_count * rg_count + slot_col % rg_count).reshape(shaped)
    mine = target == ap_here * rg_count + rg_here
    slot_from = jnp.sum(jnp.where(mine, local_slot, 0), axis=(0, 3)).reshape(devices)
    ids = jnp.arange(devices, dtype=jnp.int32)
    source = jnp.sum(
        jnp.where(slot_from[None, :] == ids[:, None], ids[None, :], 0), axis=1
    )
    send_to = lax.dynamic_slice(
        target, (0, ap_here, rg_here, 0), (ap_count, 1, 1, rg_count)
    ).reshape(devices)

    outgoing = pl.pallas_call(
        last_sums_kernel,
        out_shape=pltpu.HBM((devices, 2 * tile_rows, tile_bins), BF16),
        compiler_params=params(),
        grid_spec=pltpu.PrefetchScalarGridSpec(
            num_scalar_prefetch=1,
            in_specs=whole(1),
            out_specs=distant,
            scratch_shapes=[
                VMEM((rg_count, ap_count, 2 * tile_rows, tile_bins), BF16),
                VMEM((2, ap_count, 2 * tile_rows, LANES), F32),
                pltpu.SemaphoreType.DMA((rg_count,)),
            ],
        ),
    )(send_to, near(moved))
    incoming = lax.all_to_all(outgoing, ("ap", "rg"), split_axis=0, concat_axis=0, tiled=True)
    steps = 4
    return pl.pallas_call(
        functools.partial(place_kernel, steps),
        out_shape=shape((2, pulses, width), F32),
        compiler_params=params(),
        grid_spec=pltpu.PrefetchScalarGridSpec(
            num_scalar_prefetch=1,
            in_specs=whole(1),
            out_specs=anywhere,
            scratch_shapes=[VMEM((2, pulses, width), F32), pltpu.SemaphoreType.DMA((steps,))],
        ),
    )(source, near(incoming))


def solution(mesh):
    placed = (P(None, "ap", "rg"), P(), P(None, None, "rg"), P(None, None, "rg"), P())
    return jax.shard_map(
        per_device, mesh=mesh, in_specs=placed, out_specs=P(None, "ap", "rg"), check_vma=False
    )
```

```python
import functools
import math

import jax
import jax.numpy as jnp
from jax import lax
from jax.experimental import pallas as pl
from jax.experimental.pallas import tpu as pltpu
from jax.sharding import PartitionSpec as P

ROOT_HALF = 0.7071067811865476
LANES = 128
STEP = 8
LEAD = 64
VMEM = pltpu.VMEM
BF16 = jnp.bfloat16
F32 = jnp.float32


def whole(count):
    return [pl.BlockSpec(memory_space=VMEM)] * count


def near(value):
    return pltpu.with_memory_space_constraint(value, VMEM)


def far(value):
    return pltpu.with_memory_space_constraint(value, pltpu.HBM)


def params():
    return pltpu.CompilerParams(vmem_limit_bytes=24 * 2**20)


def at_block(block):
    return pl.ds(pl.multiple_of(block * LANES, LANES), LANES)


def split_three(values):
    high = values.astype(BF16)
    rest = values - high.astype(F32)
    middle = rest.astype(BF16)
    low = (rest - middle.astype(F32)).astype(BF16)
    return high, middle, low


def rim_kernel(
    raw_ref,
    chirp_ref,
    offset_ref,
    phase_ref,
    paired_ref,
    crossed_ref,
    near_chirp,
    near_offset,
    near_phase,
    semaphore,
):
    _, pulses, width = raw_ref.shape
    far_end = width - LANES
    odd = lax.rem(lax.axis_index("rg"), 2)
    paired_at = pl.multiple_of((1 - odd) * far_end, LANES)
    crossed_at = pl.multiple_of(odd * far_end, LANES)
    levels = offset_ref.shape[0]
    rows = 2 * levels
    copies = []
    for source, target in (
        (offset_ref, near_offset),
        (phase_ref, near_phase),
        (raw_ref.at[0, :, pl.ds(paired_at, LANES)], paired_ref.at[:pulses]),
        (raw_ref.at[1, :, pl.ds(paired_at, LANES)], paired_ref.at[pulses : 2 * pulses]),
        (raw_ref.at[0, :, pl.ds(crossed_at, LANES)], crossed_ref.at[:pulses]),
        (raw_ref.at[1, :, pl.ds(crossed_at, LANES)], crossed_ref.at[pulses : 2 * pulses]),
        (chirp_ref, near_chirp),
    ):
        copy = pltpu.make_async_copy(source, target, semaphore.at[len(copies)])
        copy.start()
        copies.append(copy)
    for copy in copies[:2]:
        copy.wait()
    for start, out_ref in ((paired_at, paired_ref), (crossed_at, crossed_ref)):
        cut = pl.ds(start, LANES)
        at = 2 * pulses
        offsets = jnp.concatenate([near_offset[l, :, cut] for l in range(levels)], axis=0)
        angles = jnp.concatenate([near_phase[l, :, cut] for l in range(levels)], axis=0)
        out_ref[at : at + rows] = offsets.astype(F32).astype(BF16)
        for part in split_three(angles):
            at += rows
            out_ref[at : at + rows] = part
    for copy in copies[2:]:
        copy.wait()


def fill_toeplitz(chirp_ref, table_ref):
    taps = chirp_ref[...].astype(BF16).astype(F32)
    zeros = jnp.zeros((1, LANES), F32)
    rolled = []
    for part in range(2):
        row = jnp.concatenate([taps[part : part + 1], zeros], axis=1)
        spread = jnp.broadcast_to(row, (LANES, 2 * LANES))
        rolled.append(pltpu.roll(spread, 0, 1, stride=1, stride_axis=0))
    real, imag = rolled
    table_ref[0] = jnp.concatenate([real, -imag], axis=0).astype(BF16)
    table_ref[1] = jnp.concatenate([imag, real], axis=0).astype(BF16)


def gathered(values, index):
    return lax.gather(
        values,
        index[:, :, None],
        lax.GatherDimensionNumbers(
            offset_dims=(),
            collapsed_slice_dims=(1,),
            start_index_map=(1,),
            operand_batching_dims=(0,),
            start_indices_batching_dims=(0,),
        ),
        slice_sizes=(1, 1),
        mode=lax.GatherScatterMode.PROMISE_IN_BOUNDS,
    )


def picked(here, following, index, beyond):
    return jnp.where(beyond, gathered(following, index), gathered(here, index))


def scaled_trig(angles):
    return jnp.cos(angles) * ROOT_HALF, jnp.sin(angles) * ROOT_HALF


def align(values, blocks, sources_of, rows_ref):
    width = values[0].shape[1]
    lanes = slice(blocks[0] * LANES, (blocks[-1] + 1) * LANES)
    count = len(blocks) * LANES
    for level, (slot, side) in enumerate(sources_of):
        shift = (width - (LANES - LEAD + STEP * (level + 1))) % width
        group, row = 2 * level // 8 * 8, 2 * level % 8
        for part in range(3):
            moved = values[part][group : group + 8]
            if shift:
                moved = pltpu.roll(moved, shift, 1)
            pair = moved[row : row + 2, :count]
            if side is None:
                rows_ref[part, slot : slot + 2, lanes] = pair
            else:
                rows_ref[part, slot : slot + 1, lanes] = jnp.where(side == 1, pair[1:2], pair[0:1])


def sources(levels, inner_levels):
    here = lax.axis_index("ap")
    return [
        (2 * level, None)
        if level < inner_levels
        else (inner_levels + level, (here >> (level - inner_levels)) & 1)
        for level in range(levels)
    ]


def compose(outer, inner, inner_beyond, lane):
    step, cos_out, sin_out = outer
    index = lane + step.astype(jnp.int32)
    beyond = index >= LANES
    index = index & (LANES - 1)
    moved, cos_in, sin_in = (
        picked(a, b, index, beyond) for a, b in zip(inner, inner_beyond)
    )
    return (
        step + moved,
        cos_out * cos_in - sin_out * sin_in,
        cos_out * sin_in + sin_out * cos_in,
    )


def steer(levels, inner_levels, blocks, rows_ref, index_ref, trig_ref):
    lane = lax.broadcasted_iota(jnp.int32, (8, LANES), 1)
    last = blocks[-1]

    def row(slot, block):
        lanes = slice(block * LANES, (block + 1) * LANES)
        return tuple(
            jnp.broadcast_to(rows_ref[part, slot : slot + 1, lanes], (8, LANES))
            for part in range(3)
        )

    sublane = lax.broadcasted_iota(jnp.int32, (8, LANES), 0)

    def operator(level):
        if level >= inner_levels:
            return {block: row(inner_levels + level, block) for block in blocks}
        upper = ((sublane >> level) & 1) == 1
        return {
            block: tuple(
                jnp.where(upper, b, a)
                for a, b in zip(row(2 * level, block), row(2 * level + 1, block))
            )
            for block in blocks
        }

    operators = [operator(level) for level in range(levels)]
    while len(operators) > 1:
        kept = blocks[:-1] if len(operators) == 2 else blocks
        joined = [
            {
                block: compose(outer[block], inner[block], inner[min(block + 1, last)], lane)
                for block in kept
            }
            for inner, outer in zip(operators[0::2], operators[1::2])
        ]
        operators = joined + operators[len(operators) // 2 * 2 :]

    for block in blocks[:-1]:
        moved, cosine, sine = operators[0][block]
        reach = lane + moved.astype(jnp.int32)
        lanes = slice(block * LANES, (block + 1) * LANES)
        index_ref[0, :, lanes] = reach & (LANES - 1)
        index_ref[1, :, lanes] = reach - LANES
        trig_ref[0, :, lanes] = cosine
        trig_ref[1, :, lanes] = sine


def combination(index_ref, trig_ref, row, lanes, rows):
    def spread(values):
        return jnp.broadcast_to(values, (rows, LANES))

    index = spread(index_ref[0, row : row + 1, lanes])
    beyond = spread(index_ref[1, row : row + 1, lanes]) >= 0
    cosine = spread(trig_ref[0, row : row + 1, lanes])
    sine = spread(trig_ref[1, row : row + 1, lanes])
    return index, beyond, cosine, sine


def term_of(here, following, steering):
    index, beyond, cosine, sine = steering
    real, imag = (picked(a, b, index, beyond) for a, b in zip(here, following))
    return real * cosine - imag * sine, real * sine + imag * cosine


def sums_and_differences(values):
    values = list(values)
    distance = 1
    while distance < len(values):
        for at in range(len(values)):
            if not at & distance:
                low, high = values[at], values[at + distance]
                values[at], values[at + distance] = low + high, low - high
        distance *= 2
    return values


def filter_block(tiles, table_ref):
    parts = [
        lax.dot_general(
            jnp.concatenate(tiles[part], axis=1),
            table_ref[part],
            (((1,), (1,)), ((), ())),
            preferred_element_type=F32,
        )
        for part in range(2)
    ]
    return parts[0] + parts[1]


def merge_first(
    levels,
    field_ref,
    here_lanes,
    next_lanes,
    lanes,
    index_ref,
    trig_ref,
    term_ref,
    out_ref,
    out_lanes,
):
    pulses = field_ref.shape[1]
    combinations = 1 << levels
    chunk = pulses // combinations
    for at in range(combinations):
        steering = combination(index_ref, trig_ref, at, lanes, chunk)
        rows = slice(at * chunk, (at + 1) * chunk)
        here = [field_ref[part, rows, here_lanes] for part in range(2)]
        following = [field_ref[part, rows, next_lanes] for part in range(2)]
        term_ref[0, at], term_ref[1, at] = term_of(here, following, steering)
    for tile in range(chunk // 8):
        cut = slice(8 * tile, 8 * tile + 8)
        real, imag = (
            sums_and_differences([term_ref[part, at, cut] for at in range(combinations)])
            for part in range(2)
        )
        for at in range(combinations):
            out_ref[at * (chunk // 8) + tile, :, out_lanes] = jnp.concatenate(
                [real[at], imag[at]], axis=0
            ).astype(BF16)


def inner_merges_kernel(
    inner_levels,
    far_raw,
    chirp_ref,
    offset_ref,
    phase_ref,
    out_ref,
    ends_ref,
    steering_ref,
    table_ref,
    raw_ref,
    loaded,
    stored,
    merged_ref,
    field_ref,
    term_ref,
    index_ref,
    trig_ref,
    rows_ref,
):
    tiles = raw_ref.shape[2] // LANES
    levels = offset_ref.shape[0]
    loading = pltpu.make_async_copy(far_raw, raw_ref, loaded.at[0])
    loading.start()
    offsets = jnp.concatenate([offset_ref[l] for l in range(levels)], axis=0)
    angles = jnp.concatenate([phase_ref[l] for l in range(levels)], axis=0)
    values = (offsets.astype(F32) + (STEP - 4.0), *scaled_trig(angles))
    for part in range(3):
        steering_ref[part] = values[part]
    blank = jnp.zeros((2 * levels, LANES), F32)
    align(
        [jnp.concatenate([blank, value, blank], axis=1) for value in values],
        range(tiles + 1),
        sources(levels, inner_levels),
        rows_ref,
    )
    steer(levels, inner_levels, range(1, tiles), rows_ref, index_ref, trig_ref)
    fill_toeplitz(chirp_ref, table_ref)
    loading.wait()
    for block in range(1, tiles):
        cut = slice((block - 1) * LANES, (block + 1) * LANES)
        both = filter_block([[raw_ref[part, :, cut]] for part in range(2)], table_ref)
        lanes = slice(block * LANES, (block + 1) * LANES)
        for part in range(2):
            values = both[:, part * LANES : (part + 1) * LANES]
            field_ref[part, :, lanes] = values
            if block == 1:
                ends_ref[part, :, :LANES] = values
            if block == tiles - 1:
                ends_ref[part, :, LANES:] = values

    def stored_block(lanes):
        return pltpu.make_async_copy(
            merged_ref.at[:, :, lanes], out_ref.at[:, :, lanes], stored.at[0]
        )

    def merge_pair(pair, carry):
        for slot in range(2):
            block = 1 + 2 * pair + slot
            lanes, beyond = at_block(block), at_block(block + 1)
            merge_first(
                inner_levels,
                field_ref,
                lanes,
                beyond,
                lanes,
                index_ref,
                trig_ref,
                term_ref.at[slot],
                merged_ref,
                lanes,
            )
        both = pl.multiple_of((1 + 2 * pair) * LANES, LANES)
        stored_block(pl.ds(both, 2 * LANES)).start()
        return carry

    lax.fori_loop(0, (tiles - 2) // 2, merge_pair, 0)
    stored_block(pl.ds(LANES, (tiles - 2) * LANES)).wait()


def outer_merges_kernel(
    inner_levels,
    total,
    partial_ref,
    ends_ref,
    steering_ref,
    raw_ref,
    paired_ref,
    crossed_ref,
    table_ref,
    out_ref,
    semaphore,
    merged_ref,
    field_ref,
    term_ref,
    index_ref,
    trig_ref,
    rows_ref,
):
    pulses, width = raw_ref.shape[1], raw_ref.shape[2]
    tiles = width // LANES
    rim_rows = steering_ref.shape[1]
    levels = rim_rows // 2
    start = lax.axis_index("rg") * width - LEAD
    own_sources = sources(levels, inner_levels)
    odd = lax.rem(lax.axis_index("rg"), 2) == 1

    def left_rim(rows):
        return jnp.where(odd, paired_ref[rows, :], crossed_ref[rows, :])

    def right_rim(rows):
        return jnp.where(odd, crossed_ref[rows, :], paired_ref[rows, :])

    def held(position):
        return slice(position * LANES, (position + 1) * LANES)

    for rim_of, at, near_lanes, blocks in (
        (left_rim, -LANES, slice(0, 2 * LANES), (0, 1)),
        (right_rim, width, slice(width - 2 * LANES, width), (tiles - 1, tiles)),
    ):
        offsets, high, middle, low = (
            rim_of(slice(2 * pulses + k * rim_rows, 2 * pulses + (k + 1) * rim_rows)).astype(F32)
            for k in range(4)
        )
        cosine, sine = scaled_trig(high + middle + low)
        bins = lax.axis_index("rg") * width + at + lax.broadcasted_iota(
            jnp.int32, (rim_rows, LANES), 1
        )
        inside = (bins >= 0) & (bins < total)
        rim = (
            offsets + (STEP - 4.0),
            jnp.where(inside, cosine, 0.0),
            jnp.where(inside, sine, 0.0),
        )
        middle = [steering_ref[part, :, near_lanes] for part in range(3)]
        joined = [
            jnp.concatenate((a, b) if at < 0 else (b, a), axis=1) for a, b in zip(rim, middle)
        ]
        align(joined, blocks, own_sources, rows_ref)
        steer(levels, inner_levels, blocks, rows_ref, index_ref, trig_ref)

    for position, block in ((0, 0), (3, tiles)):
        pair = []
        for part in range(2):
            rows = slice(part * pulses, (part + 1) * pulses)
            if block == 0:
                pair.append([left_rim(rows), raw_ref[part, :, :LANES]])
            else:
                pair.append([raw_ref[part, :, width - LANES :], right_rim(rows)])
        both = filter_block(pair, table_ref)
        bins = start + block * LANES + (lax.broadcasted_iota(jnp.int32, both.shape, 1) % LANES)
        both = jnp.where((bins >= 0) & (bins < total), both, 0.0)
        for part in range(2):
            field_ref[part, :, held(position)] = both[:, part * LANES : (part + 1) * LANES]
    for part in range(2):
        field_ref[part, :, LANES : 3 * LANES] = ends_ref[part]
    copies = []
    for here, following, block in ((0, 1, 0), (2, 3, tiles - 1)):
        merge_first(
            inner_levels,
            field_ref,
            held(here),
            held(following),
            slice(block * LANES, (block + 1) * LANES),
            index_ref,
            trig_ref,
            term_ref.at[len(copies)],
            merged_ref.at[len(copies)],
            slice(0, LANES),
        )
        copy = pltpu.make_async_copy(
            merged_ref.at[len(copies)],
            out_ref.at[:, :, pl.ds(block * LANES, LANES)],
            semaphore.at[len(copies)],
        )
        copy.start()
        copies.append(copy)
    for copy in copies:
        copy.wait()


def last_sums_kernel(target_ref, moved_ref, out_ref, tile_ref, term_ref, semaphore):
    holders, rows, columns = moved_ref.shape
    per_tile = out_ref.shape[2] // LANES
    tiles_across = columns // out_ref.shape[2]
    near_group = min(8, holders)
    for column in range(tiles_across):
        for part in range(per_tile):
            block = column * per_tile + part
            lanes = slice(block * LANES, (block + 1) * LANES)
            inner = slice(part * LANES, (part + 1) * LANES)
            slot = block % 2
            for first in range(0, holders, near_group):
                sums = sums_and_differences(
                    [moved_ref[first + at, :, lanes].astype(F32) for at in range(near_group)]
                )
                for at in range(near_group):
                    term_ref[slot, first + at] = sums[at]
            for first in range(near_group):
                members = range(first, holders, near_group)
                sums = sums_and_differences([term_ref[slot, at] for at in members])
                for at, value in zip(members, sums):
                    tile_ref[column, at, :, inner] = value.astype(BF16)
        for at in range(holders):
            to = target_ref[at * tiles_across + column]
            pltpu.make_async_copy(
                tile_ref.at[column, at], out_ref.at[to], semaphore.at[column]
            ).start()
    for column in range(tiles_across):
        pltpu.make_async_copy(
            tile_ref.at[column], out_ref.at[pl.ds(0, holders)], semaphore.at[column]
        ).wait()


def place_kernel(steps, source_ref, incoming_ref, out_ref, image_ref, semaphore):
    _, rows, width = out_ref.shape
    tile_bins = incoming_ref.shape[2]
    across = width // tile_bins
    share = rows // steps
    copies = []
    for step in range(steps):
        for row in range(step * share // 8, (step + 1) * share // 8):
            for column in range(across):
                tile = incoming_ref[source_ref[row * across + column]].astype(F32)
                for part in range(2):
                    image_ref[
                        part, row * 8 : row * 8 + 8, column * tile_bins : (column + 1) * tile_bins
                    ] = tile[8 * part : 8 * part + 8]
        cut = pl.ds(step * share, share)
        copy = pltpu.make_async_copy(
            image_ref.at[:, cut, :], out_ref.at[:, cut, :], semaphore.at[step]
        )
        copy.start()
        copies.append(copy)
    for copy in copies:
        copy.wait()


def per_device(raw_echoes, chirp, range_offsets, phases, tile_table):
    ap_count, rg_count = lax.axis_size("ap"), lax.axis_size("rg")
    devices = ap_count * rg_count
    _, pulses, width = raw_echoes.shape
    level_count = range_offsets.shape[0]
    total = width * rg_count
    outer_levels = ap_count.bit_length() - 1
    inner_levels = level_count - outer_levels
    tile_rows = pulses // ap_count
    tile_bins = width // rg_count
    rim_rows = 2 * pulses + 8 * level_count
    shape = jax.ShapeDtypeStruct

    anywhere = pl.BlockSpec(memory_space=pl.ANY)
    distant = pl.BlockSpec(memory_space=pltpu.HBM)
    to_paired, to_crossed, near_chirp, near_offsets, near_phases = pl.pallas_call(
        rim_kernel,
        out_shape=[VMEM((rim_rows, LANES), BF16)] * 2
        + [
            VMEM(chirp.shape, F32),
            VMEM(range_offsets.shape, jnp.int32),
            VMEM(phases.shape, F32),
        ],
        compiler_params=params(),
        in_specs=[distant] * 4,
        out_specs=whole(5),
        scratch_shapes=[pltpu.SemaphoreType.DMA((7,))],
    )(*map(far, (raw_echoes, chirp, range_offsets, phases)))
    from_paired = lax.ppermute(to_paired, "rg", [(i, i ^ 1) for i in range(rg_count)])
    crossed_pairs = [(i, i + 1) for i in range(1, rg_count - 1, 2)]
    from_crossed = lax.ppermute(
        to_crossed, "rg", crossed_pairs + [(j, i) for i, j in crossed_pairs]
    )
    inner = 1 << inner_levels
    merged_shape = pltpu.HBM((ap_count, 2 * tile_rows, width), BF16)

    def first_scratch(held):
        return [
            VMEM((2, pulses, held), F32),
            VMEM((2, 2, inner, pulses // inner, LANES), F32),
            VMEM((2, inner, width), jnp.int32),
            VMEM((2, inner, width), F32),
            VMEM((3, inner_levels + level_count, width + LANES), F32),
        ]

    partial, field_ends, steering, table, near_raw = pl.pallas_call(
        functools.partial(inner_merges_kernel, inner_levels),
        out_shape=[
            merged_shape,
            VMEM((2, pulses, 2 * LANES), F32),
            VMEM((3, 2 * level_count, width), F32),
            VMEM((2, 2 * LANES, 2 * LANES), BF16),
            VMEM(raw_echoes.shape, BF16),
        ],
        compiler_params=params(),
        in_specs=[distant] + whole(3),
        out_specs=[distant] + whole(4),
        scratch_shapes=[
            pltpu.SemaphoreType.DMA((1,)),
            pltpu.SemaphoreType.DMA((1,)),
            VMEM((ap_count, 2 * tile_rows, width), BF16),
        ]
        + first_scratch(width),
    )(far(raw_echoes), *map(near, (near_chirp, near_offsets, near_phases)))
    merged = pl.pallas_call(
        functools.partial(outer_merges_kernel, inner_levels, total),
        out_shape=merged_shape,
        compiler_params=params(),
        in_specs=[distant] + whole(6),
        out_specs=distant,
        input_output_aliases={0: 0},
        scratch_shapes=[
            pltpu.SemaphoreType.DMA((2,)),
            VMEM((2, ap_count, 2 * tile_rows, LANES), BF16),
        ]
        + first_scratch(4 * LANES),
    )(
        far(partial),
        *map(near, (field_ends, steering, near_raw, from_paired, from_crossed, table)),
    )
    moved = lax.all_to_all(merged, "ap", split_axis=0, concat_axis=0, tiled=True)

    ap_here, rg_here = lax.axis_index("ap"), lax.axis_index("rg")
    slot_row = tile_table // (rg_count * rg_count)
    slot_col = tile_table % (rg_count * rg_count)
    target = slot_row // ap_count * rg_count + slot_col // rg_count
    shaped = (ap_count, ap_count, rg_count, rg_count)
    target = target.reshape(shaped)
    local_slot = (slot_row % ap_count * rg_count + slot_col % rg_count).reshape(shaped)
    mine = target == ap_here * rg_count + rg_here
    slot_from = jnp.sum(jnp.where(mine, local_slot, 0), axis=(0, 3)).reshape(devices)
    ids = jnp.arange(devices, dtype=jnp.int32)
    source = jnp.sum(
        jnp.where(slot_from[None, :] == ids[:, None], ids[None, :], 0), axis=1
    )
    send_to = lax.dynamic_slice(
        target, (0, ap_here, rg_here, 0), (ap_count, 1, 1, rg_count)
    ).reshape(devices)

    outgoing = pl.pallas_call(
        last_sums_kernel,
        out_shape=pltpu.HBM((devices, 2 * tile_rows, tile_bins), BF16),
        compiler_params=params(),
        grid_spec=pltpu.PrefetchScalarGridSpec(
            num_scalar_prefetch=1,
            in_specs=whole(1),
            out_specs=distant,
            scratch_shapes=[
                VMEM((rg_count, ap_count, 2 * tile_rows, tile_bins), BF16),
                VMEM((2, ap_count, 2 * tile_rows, LANES), F32),
                pltpu.SemaphoreType.DMA((rg_count,)),
            ],
        ),
    )(send_to, near(moved))
    incoming = lax.all_to_all(outgoing, ("ap", "rg"), split_axis=0, concat_axis=0, tiled=True)
    steps = 8
    return pl.pallas_call(
        functools.partial(place_kernel, steps),
        out_shape=shape((2, pulses, width), F32),
        compiler_params=params(),
        grid_spec=pltpu.PrefetchScalarGridSpec(
            num_scalar_prefetch=1,
            in_specs=whole(1),
            out_specs=anywhere,
            scratch_shapes=[VMEM((2, pulses, width), F32), pltpu.SemaphoreType.DMA((steps,))],
        ),
    )(source, near(incoming))


def solution(mesh):
    placed = (P(None, "ap", "rg"), P(), P(None, None, "rg"), P(None, None, "rg"), P())
    return jax.shard_map(
        per_device, mesh=mesh, in_specs=placed, out_specs=P(None, "ap", "rg"), check_vma=False
    )
```

```python
import functools
import math

import jax
import jax.numpy as jnp
from jax import lax
from jax.experimental import pallas as pl
from jax.experimental.pallas import tpu as pltpu
from jax.sharding import PartitionSpec as P

ROOT_HALF = 0.7071067811865476
LANES = 128
STEP = 8
LEAD = 64
VMEM = pltpu.VMEM
BF16 = jnp.bfloat16
F32 = jnp.float32


def whole(count):
    return [pl.BlockSpec(memory_space=VMEM)] * count


def near(value):
    return pltpu.with_memory_space_constraint(value, VMEM)


def far(value):
    return pltpu.with_memory_space_constraint(value, pltpu.HBM)


def params():
    return pltpu.CompilerParams(vmem_limit_bytes=24 * 2**20)


def at_block(block):
    return pl.ds(pl.multiple_of(block * LANES, LANES), LANES)


def split_three(values):
    high = values.astype(BF16)
    rest = values - high.astype(F32)
    middle = rest.astype(BF16)
    low = (rest - middle.astype(F32)).astype(BF16)
    return high, middle, low


def rim_kernel(
    raw_ref,
    chirp_ref,
    offset_ref,
    phase_ref,
    paired_ref,
    crossed_ref,
    near_chirp,
    near_offset,
    near_phase,
    near_raw,
    semaphore,
):
    _, pulses, width = raw_ref.shape
    far_end = width - LANES
    odd = lax.rem(lax.axis_index("rg"), 2)
    paired_at = pl.multiple_of((1 - odd) * far_end, LANES)
    crossed_at = pl.multiple_of(odd * far_end, LANES)
    levels = offset_ref.shape[0]
    rows = 2 * levels
    copies = []
    for source, target in (
        (offset_ref, near_offset),
        (phase_ref, near_phase),
        (raw_ref.at[0, :, pl.ds(paired_at, LANES)], paired_ref.at[:pulses]),
        (raw_ref.at[1, :, pl.ds(paired_at, LANES)], paired_ref.at[pulses : 2 * pulses]),
        (raw_ref.at[0, :, pl.ds(crossed_at, LANES)], crossed_ref.at[:pulses]),
        (raw_ref.at[1, :, pl.ds(crossed_at, LANES)], crossed_ref.at[pulses : 2 * pulses]),
        (chirp_ref, near_chirp),
        (raw_ref, near_raw),
    ):
        copy = pltpu.make_async_copy(source, target, semaphore.at[len(copies)])
        copy.start()
        copies.append(copy)
    for copy in copies[:2]:
        copy.wait()
    for start, out_ref in ((paired_at, paired_ref), (crossed_at, crossed_ref)):
        cut = pl.ds(start, LANES)
        at = 2 * pulses
        offsets, angles = by_side(near_offset, cut), by_side(near_phase, cut)
        out_ref[at : at + rows] = offsets.astype(F32).astype(BF16)
        for part in split_three(angles):
            at += rows
            out_ref[at : at + rows] = part
    for copy in copies[2:]:
        copy.wait()


def fill_toeplitz(chirp_ref, table_ref):
    taps = chirp_ref[...].astype(BF16).astype(F32)
    zeros = jnp.zeros((1, LANES), F32)
    rolled = []
    for part in range(2):
        row = jnp.concatenate([taps[part : part + 1], zeros], axis=1)
        spread = jnp.broadcast_to(row, (LANES, 2 * LANES))
        rolled.append(pltpu.roll(spread, 0, 1, stride=1, stride_axis=0))
    real, imag = rolled
    table_ref[0] = jnp.concatenate([real, -imag], axis=0).astype(BF16)
    table_ref[1] = jnp.concatenate([imag, real], axis=0).astype(BF16)


def gathered(values, index):
    return lax.gather(
        values,
        index[:, :, None],
        lax.GatherDimensionNumbers(
            offset_dims=(),
            collapsed_slice_dims=(1,),
            start_index_map=(1,),
            operand_batching_dims=(0,),
            start_indices_batching_dims=(0,),
        ),
        slice_sizes=(1, 1),
        mode=lax.GatherScatterMode.PROMISE_IN_BOUNDS,
    )


def picked(here, following, index, beyond):
    return jnp.where(beyond, gathered(following, index), gathered(here, index))


def scaled_trig(angles):
    return jnp.cos(angles) * ROOT_HALF, jnp.sin(angles) * ROOT_HALF


def by_side(ref, lanes):
    levels = ref.shape[0]
    return jnp.concatenate(
        [ref[level, side : side + 1, lanes] for side in range(2) for level in reversed(range(levels))],
        axis=0,
    )


def align(values, inner_levels, blocks, rows_ref):
    rows, width = values[0].shape
    levels = rows // 2
    lanes = slice(blocks[0] * LANES, (blocks[-1] + 1) * LANES)
    count = len(blocks) * LANES
    level = levels - 1 - lax.broadcasted_iota(jnp.int32, (levels, count), 0)
    bit = jnp.left_shift(1, jnp.maximum(level - inner_levels, 0))
    upper = (lax.axis_index("ap") & bit) != 0
    for part in range(3):
        sides = [
            pltpu.roll(
                values[part][side * levels : (side + 1) * levels],
                width - (LEAD + STEP * levels),
                1,
                stride=STEP,
                stride_axis=0,
            )[:, :count]
            for side in range(2)
        ]
        for at, moved in enumerate(sides + [jnp.where(upper, sides[1], sides[0])]):
            rows_ref[part, at * levels : (at + 1) * levels, lanes] = moved


def compose(outer, inner, inner_beyond, lane):
    step, cos_out, sin_out = outer
    index = lane + step.astype(jnp.int32)
    beyond = index >= LANES
    index = index & (LANES - 1)
    moved, cos_in, sin_in = (
        picked(a, b, index, beyond) for a, b in zip(inner, inner_beyond)
    )
    return (
        step + moved,
        cos_out * cos_in - sin_out * sin_in,
        cos_out * sin_in + sin_out * cos_in,
    )


def steer(levels, inner_levels, blocks, rows_ref, index_ref, trig_ref):
    lane = lax.broadcasted_iota(jnp.int32, (8, LANES), 1)
    last = blocks[-1]

    def row(slot, block):
        lanes = slice(block * LANES, (block + 1) * LANES)
        return tuple(
            jnp.broadcast_to(rows_ref[part, slot : slot + 1, lanes], (8, LANES))
            for part in range(3)
        )

    sublane = lax.broadcasted_iota(jnp.int32, (8, LANES), 0)

    def operator(level):
        slot = levels - 1 - level
        if level >= inner_levels:
            return {block: row(2 * levels + slot, block) for block in blocks}
        upper = ((sublane >> level) & 1) == 1
        return {
            block: tuple(
                jnp.where(upper, b, a)
                for a, b in zip(row(slot, block), row(levels + slot, block))
            )
            for block in blocks
        }

    operators = [operator(level) for level in range(levels)]
    while len(operators) > 1:
        kept = blocks[:-1] if len(operators) == 2 else blocks
        joined = [
            {
                block: compose(outer[block], inner[block], inner[min(block + 1, last)], lane)
                for block in kept
            }
            for inner, outer in zip(operators[0::2], operators[1::2])
        ]
        operators = joined + operators[len(operators) // 2 * 2 :]

    for block in blocks[:-1]:
        moved, cosine, sine = operators[0][block]
        reach = lane + moved.astype(jnp.int32)
        lanes = slice(block * LANES, (block + 1) * LANES)
        index_ref[0, :, lanes] = reach & (LANES - 1)
        index_ref[1, :, lanes] = reach - LANES
        trig_ref[0, :, lanes] = cosine
        trig_ref[1, :, lanes] = sine


def combination(index_ref, trig_ref, row, lanes, rows):
    def spread(values):
        return jnp.broadcast_to(values, (rows, LANES))

    index = spread(index_ref[0, row : row + 1, lanes])
    beyond = spread(index_ref[1, row : row + 1, lanes]) >= 0
    cosine = spread(trig_ref[0, row : row + 1, lanes])
    sine = spread(trig_ref[1, row : row + 1, lanes])
    return index, beyond, cosine, sine


def term_of(here, following, steering):
    index, beyond, cosine, sine = steering
    real, imag = (picked(a, b, index, beyond) for a, b in zip(here, following))
    return real * cosine - imag * sine, real * sine + imag * cosine


def sums_and_differences(values):
    values = list(values)
    distance = 1
    while distance < len(values):
        for at in range(len(values)):
            if not at & distance:
                low, high = values[at], values[at + distance]
                values[at], values[at + distance] = low + high, low - high
        distance *= 2
    return values


def filter_block(tiles, table_ref):
    parts = [
        lax.dot_general(
            jnp.concatenate(tiles[part], axis=1),
            table_ref[part],
            (((1,), (1,)), ((), ())),
            preferred_element_type=F32,
        )
        for part in range(2)
    ]
    return parts[0] + parts[1]


def merge_first(
    levels,
    field_ref,
    here_lanes,
    next_lanes,
    lanes,
    index_ref,
    trig_ref,
    term_ref,
    out_ref,
    out_lanes,
):
    pulses = field_ref.shape[1]
    combinations = 1 << levels
    chunk = pulses // combinations
    for at in range(combinations):
        steering = combination(index_ref, trig_ref, at, lanes, chunk)
        rows = slice(at * chunk, (at + 1) * chunk)
        here = [field_ref[part, rows, here_lanes] for part in range(2)]
        following = [field_ref[part, rows, next_lanes] for part in range(2)]
        term_ref[0, at], term_ref[1, at] = term_of(here, following, steering)
    for tile in range(chunk // 8):
        cut = slice(8 * tile, 8 * tile + 8)
        real, imag = (
            sums_and_differences([term_ref[part, at, cut] for at in range(combinations)])
            for part in range(2)
        )
        for at in range(combinations):
            out_ref[at * (chunk // 8) + tile, :, out_lanes] = jnp.concatenate(
                [real[at], imag[at]], axis=0
            ).astype(BF16)


def inner_merges_kernel(
    inner_levels,
    raw_ref,
    chirp_ref,
    offset_ref,
    phase_ref,
    out_ref,
    ends_ref,
    steering_ref,
    table_ref,
    stored,
    merged_ref,
    field_ref,
    term_ref,
    index_ref,
    trig_ref,
    rows_ref,
):
    tiles = raw_ref.shape[2] // LANES
    levels = offset_ref.shape[0]
    offsets, angles = (by_side(ref, slice(None)) for ref in (offset_ref, phase_ref))
    values = (offsets.astype(F32) + (STEP - 4.0), *scaled_trig(angles))
    for part in range(3):
        steering_ref[part] = values[part]
    blank = jnp.zeros((2 * levels, LANES), F32)
    align(
        [jnp.concatenate([blank, value, blank], axis=1) for value in values],
        inner_levels,
        range(tiles + 1),
        rows_ref,
    )
    steer(levels, inner_levels, range(1, tiles), rows_ref, index_ref, trig_ref)
    fill_toeplitz(chirp_ref, table_ref)
    for block in range(1, tiles):
        cut = slice((block - 1) * LANES, (block + 1) * LANES)
        both = filter_block([[raw_ref[part, :, cut]] for part in range(2)], table_ref)
        lanes = slice(block * LANES, (block + 1) * LANES)
        for part in range(2):
            values = both[:, part * LANES : (part + 1) * LANES]
            field_ref[part, :, lanes] = values
            if block == 1:
                ends_ref[part, :, :LANES] = values
            if block == tiles - 1:
                ends_ref[part, :, LANES:] = values

    def stored_block(lanes):
        return pltpu.make_async_copy(
            merged_ref.at[:, :, lanes], out_ref.at[:, :, lanes], stored.at[0]
        )

    def merge_pair(pair, carry):
        for slot in range(2):
            block = 1 + 2 * pair + slot
            lanes, beyond = at_block(block), at_block(block + 1)
            merge_first(
                inner_levels,
                field_ref,
                lanes,
                beyond,
                lanes,
                index_ref,
                trig_ref,
                term_ref.at[slot],
                merged_ref,
                lanes,
            )
        both = pl.multiple_of((1 + 2 * pair) * LANES, LANES)
        stored_block(pl.ds(both, 2 * LANES)).start()
        return carry

    lax.fori_loop(0, (tiles - 2) // 2, merge_pair, 0)
    stored_block(pl.ds(LANES, (tiles - 2) * LANES)).wait()


def outer_merges_kernel(
    inner_levels,
    total,
    partial_ref,
    ends_ref,
    steering_ref,
    raw_ref,
    paired_ref,
    crossed_ref,
    table_ref,
    out_ref,
    semaphore,
    merged_ref,
    field_ref,
    term_ref,
    index_ref,
    trig_ref,
    rows_ref,
):
    pulses, width = raw_ref.shape[1], raw_ref.shape[2]
    tiles = width // LANES
    rim_rows = steering_ref.shape[1]
    levels = rim_rows // 2
    start = lax.axis_index("rg") * width - LEAD
    odd = lax.rem(lax.axis_index("rg"), 2) == 1

    def left_rim(rows):
        return jnp.where(odd, paired_ref[rows, :], crossed_ref[rows, :])

    def right_rim(rows):
        return jnp.where(odd, crossed_ref[rows, :], paired_ref[rows, :])

    def held(position):
        return slice(position * LANES, (position + 1) * LANES)

    for rim_of, at, near_lanes, blocks in (
        (left_rim, -LANES, slice(0, 2 * LANES), (0, 1)),
        (right_rim, width, slice(width - 2 * LANES, width), (tiles - 1, tiles)),
    ):
        offsets, high, middle, low = (
            rim_of(slice(2 * pulses + k * rim_rows, 2 * pulses + (k + 1) * rim_rows)).astype(F32)
            for k in range(4)
        )
        cosine, sine = scaled_trig(high + middle + low)
        bins = lax.axis_index("rg") * width + at + lax.broadcasted_iota(
            jnp.int32, (rim_rows, LANES), 1
        )
        inside = (bins >= 0) & (bins < total)
        rim = (
            offsets + (STEP - 4.0),
            jnp.where(inside, cosine, 0.0),
            jnp.where(inside, sine, 0.0),
        )
        middle = [steering_ref[part, :, near_lanes] for part in range(3)]
        joined = [
            jnp.concatenate((a, b) if at < 0 else (b, a), axis=1) for a, b in zip(rim, middle)
        ]
        align(joined, inner_levels, blocks, rows_ref)
        steer(levels, inner_levels, blocks, rows_ref, index_ref, trig_ref)

    for position, block in ((0, 0), (3, tiles)):
        pair = []
        for part in range(2):
            rows = slice(part * pulses, (part + 1) * pulses)
            if block == 0:
                pair.append([left_rim(rows), raw_ref[part, :, :LANES]])
            else:
                pair.append([raw_ref[part, :, width - LANES :], right_rim(rows)])
        both = filter_block(pair, table_ref)
        bins = start + block * LANES + (lax.broadcasted_iota(jnp.int32, both.shape, 1) % LANES)
        both = jnp.where((bins >= 0) & (bins < total), both, 0.0)
        for part in range(2):
            field_ref[part, :, held(position)] = both[:, part * LANES : (part + 1) * LANES]
    for part in range(2):
        field_ref[part, :, LANES : 3 * LANES] = ends_ref[part]
    copies = []
    for here, following, block in ((0, 1, 0), (2, 3, tiles - 1)):
        merge_first(
            inner_levels,
            field_ref,
            held(here),
            held(following),
            slice(block * LANES, (block + 1) * LANES),
            index_ref,
            trig_ref,
            term_ref.at[len(copies)],
            merged_ref.at[len(copies)],
            slice(0, LANES),
        )
        copy = pltpu.make_async_copy(
            merged_ref.at[len(copies)],
            out_ref.at[:, :, pl.ds(block * LANES, LANES)],
            semaphore.at[len(copies)],
        )
        copy.start()
        copies.append(copy)
    for copy in copies:
        copy.wait()


def last_sums_kernel(target_ref, moved_ref, out_ref, tile_ref, term_ref, semaphore):
    holders, rows, columns = moved_ref.shape
    per_tile = out_ref.shape[2] // LANES
    tiles_across = columns // out_ref.shape[2]
    near_group = min(8, holders)
    for column in range(tiles_across):
        for part in range(per_tile):
            block = column * per_tile + part
            lanes = slice(block * LANES, (block + 1) * LANES)
            inner = slice(part * LANES, (part + 1) * LANES)
            slot = block % 2
            for first in range(0, holders, near_group):
                sums = sums_and_differences(
                    [moved_ref[first + at, :, lanes].astype(F32) for at in range(near_group)]
                )
                for at in range(near_group):
                    term_ref[slot, first + at] = sums[at]
            for first in range(near_group):
                members = range(first, holders, near_group)
                sums = sums_and_differences([term_ref[slot, at] for at in members])
                for at, value in zip(members, sums):
                    tile_ref[column, at, :, inner] = value.astype(BF16)
        for at in range(holders):
            to = target_ref[at * tiles_across + column]
            pltpu.make_async_copy(
                tile_ref.at[column, at], out_ref.at[to], semaphore.at[column]
            ).start()
    for column in range(tiles_across):
        pltpu.make_async_copy(
            tile_ref.at[column], out_ref.at[pl.ds(0, holders)], semaphore.at[column]
        ).wait()


def place_kernel(steps, source_ref, incoming_ref, out_ref, image_ref, semaphore):
    _, rows, width = out_ref.shape
    tile_bins = incoming_ref.shape[2]
    across = width // tile_bins
    share = rows // steps
    copies = []
    for step in range(steps):
        for row in range(step * share // 8, (step + 1) * share // 8):
            for column in range(across):
                tile = incoming_ref[source_ref[row * across + column]].astype(F32)
                for part in range(2):
                    image_ref[
                        part, row * 8 : row * 8 + 8, column * tile_bins : (column + 1) * tile_bins
                    ] = tile[8 * part : 8 * part + 8]
        cut = pl.ds(step * share, share)
        copy = pltpu.make_async_copy(
            image_ref.at[:, cut, :], out_ref.at[:, cut, :], semaphore.at[step]
        )
        copy.start()
        copies.append(copy)
    for copy in copies:
        copy.wait()


def per_device(raw_echoes, chirp, range_offsets, phases, tile_table):
    ap_count, rg_count = lax.axis_size("ap"), lax.axis_size("rg")
    devices = ap_count * rg_count
    _, pulses, width = raw_echoes.shape
    level_count = range_offsets.shape[0]
    total = width * rg_count
    outer_levels = ap_count.bit_length() - 1
    inner_levels = level_count - outer_levels
    tile_rows = pulses // ap_count
    tile_bins = width // rg_count
    rim_rows = 2 * pulses + 8 * level_count
    shape = jax.ShapeDtypeStruct

    anywhere = pl.BlockSpec(memory_space=pl.ANY)
    distant = pl.BlockSpec(memory_space=pltpu.HBM)
    to_paired, to_crossed, near_chirp, near_offsets, near_phases, near_raw = pl.pallas_call(
        rim_kernel,
        out_shape=[VMEM((rim_rows, LANES), BF16)] * 2
        + [
            VMEM(chirp.shape, F32),
            VMEM(range_offsets.shape, jnp.int32),
            VMEM(phases.shape, F32),
            VMEM(raw_echoes.shape, BF16),
        ],
        compiler_params=params(),
        in_specs=[distant] * 4,
        out_specs=whole(6),
        scratch_shapes=[pltpu.SemaphoreType.DMA((8,))],
    )(*map(far, (raw_echoes, chirp, range_offsets, phases)))
    from_paired = lax.ppermute(to_paired, "rg", [(i, i ^ 1) for i in range(rg_count)])
    crossed_pairs = [(i, i + 1) for i in range(1, rg_count - 1, 2)]
    from_crossed = lax.ppermute(
        to_crossed, "rg", crossed_pairs + [(j, i) for i, j in crossed_pairs]
    )
    inner = 1 << inner_levels
    merged_shape = pltpu.HBM((ap_count, 2 * tile_rows, width), BF16)

    def first_scratch(held):
        return [
            VMEM((2, pulses, held), F32),
            VMEM((2, 2, inner, pulses // inner, LANES), F32),
            VMEM((2, inner, width), jnp.int32),
            VMEM((2, inner, width), F32),
            VMEM((3, 3 * level_count, width + LANES), F32),
        ]

    partial, field_ends, steering, table = pl.pallas_call(
        functools.partial(inner_merges_kernel, inner_levels),
        out_shape=[
            merged_shape,
            VMEM((2, pulses, 2 * LANES), F32),
            VMEM((3, 2 * level_count, width), F32),
            VMEM((2, 2 * LANES, 2 * LANES), BF16),
        ],
        compiler_params=params(),
        in_specs=whole(4),
        out_specs=[distant] + whole(3),
        scratch_shapes=[
            pltpu.SemaphoreType.DMA((1,)),
            VMEM((ap_count, 2 * tile_rows, width), BF16),
        ]
        + first_scratch(width),
    )(*map(near, (near_raw, near_chirp, near_offsets, near_phases)))
    merged = pl.pallas_call(
        functools.partial(outer_merges_kernel, inner_levels, total),
        out_shape=merged_shape,
        compiler_params=params(),
        in_specs=[distant] + whole(6),
        out_specs=distant,
        input_output_aliases={0: 0},
        scratch_shapes=[
            pltpu.SemaphoreType.DMA((2,)),
            VMEM((2, ap_count, 2 * tile_rows, LANES), BF16),
        ]
        + first_scratch(4 * LANES),
    )(
        far(partial),
        *map(near, (field_ends, steering, near_raw, from_paired, from_crossed, table)),
    )
    moved = lax.all_to_all(merged, "ap", split_axis=0, concat_axis=0, tiled=True)

    ap_here, rg_here = lax.axis_index("ap"), lax.axis_index("rg")
    slot_row = tile_table // (rg_count * rg_count)
    slot_col = tile_table % (rg_count * rg_count)
    target = slot_row // ap_count * rg_count + slot_col // rg_count
    shaped = (ap_count, ap_count, rg_count, rg_count)
    target = target.reshape(shaped)
    local_slot = (slot_row % ap_count * rg_count + slot_col % rg_count).reshape(shaped)
    mine = target == ap_here * rg_count + rg_here
    slot_from = jnp.sum(jnp.where(mine, local_slot, 0), axis=(0, 3)).reshape(devices)
    ids = jnp.arange(devices, dtype=jnp.int32)
    source = jnp.sum(
        jnp.where(slot_from[None, :] == ids[:, None], ids[None, :], 0), axis=1
    )
    send_to = lax.dynamic_slice(
        target, (0, ap_here, rg_here, 0), (ap_count, 1, 1, rg_count)
    ).reshape(devices)

    outgoing = pl.pallas_call(
        last_sums_kernel,
        out_shape=pltpu.HBM((devices, 2 * tile_rows, tile_bins), BF16),
        compiler_params=params(),
        grid_spec=pltpu.PrefetchScalarGridSpec(
            num_scalar_prefetch=1,
            in_specs=whole(1),
            out_specs=distant,
            scratch_shapes=[
                VMEM((rg_count, ap_count, 2 * tile_rows, tile_bins), BF16),
                VMEM((2, ap_count, 2 * tile_rows, LANES), F32),
                pltpu.SemaphoreType.DMA((rg_count,)),
            ],
        ),
    )(send_to, near(moved))
    incoming = lax.all_to_all(outgoing, ("ap", "rg"), split_axis=0, concat_axis=0, tiled=True)
    steps = 8
    return pl.pallas_call(
        functools.partial(place_kernel, steps),
        out_shape=shape((2, pulses, width), F32),
        compiler_params=params(),
        grid_spec=pltpu.PrefetchScalarGridSpec(
            num_scalar_prefetch=1,
            in_specs=whole(1),
            out_specs=anywhere,
            scratch_shapes=[VMEM((2, pulses, width), F32), pltpu.SemaphoreType.DMA((steps,))],
        ),
    )(source, near(incoming))


def solution(mesh):
    placed = (P(None, "ap", "rg"), P(), P(None, None, "rg"), P(None, None, "rg"), P())
    return jax.shard_map(
        per_device, mesh=mesh, in_specs=placed, out_specs=P(None, "ap", "rg"), check_vma=False
    )
```

```python
import functools
import math

import jax
import jax.numpy as jnp
from jax import lax
from jax.experimental import pallas as pl
from jax.experimental.pallas import tpu as pltpu
from jax.sharding import PartitionSpec as P

ROOT_HALF = 0.7071067811865476
LANES = 128
STEP = 8
LEAD = 64
VMEM = pltpu.VMEM
BF16 = jnp.bfloat16
F32 = jnp.float32


def whole(count):
    return [pl.BlockSpec(memory_space=VMEM)] * count


def near(value):
    return pltpu.with_memory_space_constraint(value, VMEM)


def far(value):
    return pltpu.with_memory_space_constraint(value, pltpu.HBM)


def params():
    return pltpu.CompilerParams(vmem_limit_bytes=24 * 2**20)


def at_block(block):
    return pl.ds(pl.multiple_of(block * LANES, LANES), LANES)


def split_three(values):
    high = values.astype(BF16)
    rest = values - high.astype(F32)
    middle = rest.astype(BF16)
    low = (rest - middle.astype(F32)).astype(BF16)
    return high, middle, low


def rim_kernel(
    raw_ref,
    chirp_ref,
    offset_ref,
    phase_ref,
    paired_ref,
    crossed_ref,
    near_chirp,
    near_offset,
    near_phase,
    near_raw,
    semaphore,
):
    _, pulses, width = raw_ref.shape
    far_end = width - LANES
    odd = lax.rem(lax.axis_index("rg"), 2)
    paired_at = pl.multiple_of((1 - odd) * far_end, LANES)
    crossed_at = pl.multiple_of(odd * far_end, LANES)
    levels = offset_ref.shape[0]
    rows = 2 * levels
    copies = []
    for source, target in (
        (offset_ref, near_offset),
        (phase_ref, near_phase),
        (raw_ref.at[0, :, pl.ds(paired_at, LANES)], paired_ref.at[:pulses]),
        (raw_ref.at[1, :, pl.ds(paired_at, LANES)], paired_ref.at[pulses : 2 * pulses]),
        (raw_ref.at[0, :, pl.ds(crossed_at, LANES)], crossed_ref.at[:pulses]),
        (raw_ref.at[1, :, pl.ds(crossed_at, LANES)], crossed_ref.at[pulses : 2 * pulses]),
        (chirp_ref, near_chirp),
        (raw_ref, near_raw),
    ):
        copy = pltpu.make_async_copy(source, target, semaphore.at[len(copies)])
        copy.start()
        copies.append(copy)
    for copy in copies[:2]:
        copy.wait()
    for start, out_ref in ((paired_at, paired_ref), (crossed_at, crossed_ref)):
        cut = pl.ds(start, LANES)
        at = 2 * pulses
        offsets, angles = by_side(near_offset, cut), by_side(near_phase, cut)
        out_ref[at : at + rows] = offsets.astype(F32).astype(BF16)
        for part in split_three(angles):
            at += rows
            out_ref[at : at + rows] = part
    for copy in copies[2:]:
        copy.wait()


def fill_toeplitz(chirp_ref, table_ref):
    taps = chirp_ref[...].astype(BF16).astype(F32)
    zeros = jnp.zeros((1, LANES), F32)
    rolled = []
    for part in range(2):
        row = jnp.concatenate([taps[part : part + 1], zeros], axis=1)
        spread = jnp.broadcast_to(row, (LANES, 2 * LANES))
        rolled.append(pltpu.roll(spread, 0, 1, stride=1, stride_axis=0))
    real, imag = rolled
    table_ref[0] = jnp.concatenate([real, -imag], axis=0).astype(BF16)
    table_ref[1] = jnp.concatenate([imag, real], axis=0).astype(BF16)


def gathered(values, index):
    return lax.gather(
        values,
        index[:, :, None],
        lax.GatherDimensionNumbers(
            offset_dims=(),
            collapsed_slice_dims=(1,),
            start_index_map=(1,),
            operand_batching_dims=(0,),
            start_indices_batching_dims=(0,),
        ),
        slice_sizes=(1, 1),
        mode=lax.GatherScatterMode.PROMISE_IN_BOUNDS,
    )


def picked(here, following, index, beyond):
    return jnp.where(beyond, gathered(following, index), gathered(here, index))


def scaled_trig(angles):
    return jnp.cos(angles) * ROOT_HALF, jnp.sin(angles) * ROOT_HALF


def by_side(ref, lanes):
    levels = ref.shape[0]
    return jnp.concatenate(
        [ref[level, side : side + 1, lanes] for side in range(2) for level in reversed(range(levels))],
        axis=0,
    )


def align(values, inner_levels, blocks, rows_ref):
    rows, width = values[0].shape
    levels = rows // 2
    lanes = slice(blocks[0] * LANES, (blocks[-1] + 1) * LANES)
    count = len(blocks) * LANES
    level = levels - 1 - lax.broadcasted_iota(jnp.int32, (levels, count), 0)
    bit = jnp.left_shift(1, jnp.maximum(level - inner_levels, 0))
    upper = (lax.axis_index("ap") & bit) != 0
    for part in range(3):
        sides = [
            pltpu.roll(
                values[part][side * levels : (side + 1) * levels],
                width - (LEAD + STEP * levels),
                1,
                stride=STEP,
                stride_axis=0,
            )[:, :count]
            for side in range(2)
        ]
        for at, moved in enumerate(sides + [jnp.where(upper, sides[1], sides[0])]):
            rows_ref[part, at * levels : (at + 1) * levels, lanes] = moved


def compose(outer, inner, inner_beyond, lane):
    step, cos_out, sin_out = outer
    index = lane + step.astype(jnp.int32)
    beyond = index >= LANES
    index = index & (LANES - 1)
    moved, cos_in, sin_in = (
        picked(a, b, index, beyond) for a, b in zip(inner, inner_beyond)
    )
    return (
        step + moved,
        cos_out * cos_in - sin_out * sin_in,
        cos_out * sin_in + sin_out * cos_in,
    )


def steer(levels, inner_levels, blocks, rows_ref, index_ref, trig_ref):
    lane = lax.broadcasted_iota(jnp.int32, (8, LANES), 1)
    last = blocks[-1]

    def row(slot, block):
        lanes = slice(block * LANES, (block + 1) * LANES)
        return tuple(
            jnp.broadcast_to(rows_ref[part, slot : slot + 1, lanes], (8, LANES))
            for part in range(3)
        )

    sublane = lax.broadcasted_iota(jnp.int32, (8, LANES), 0)

    def operator(level):
        slot = levels - 1 - level
        if level >= inner_levels:
            return {block: row(2 * levels + slot, block) for block in blocks}
        upper = ((sublane >> level) & 1) == 1
        return {
            block: tuple(
                jnp.where(upper, b, a)
                for a, b in zip(row(slot, block), row(levels + slot, block))
            )
            for block in blocks
        }

    operators = [operator(level) for level in range(levels)]
    while len(operators) > 1:
        kept = blocks[:-1] if len(operators) == 2 else blocks
        joined = [
            {
                block: compose(outer[block], inner[block], inner[min(block + 1, last)], lane)
                for block in kept
            }
            for inner, outer in zip(operators[0::2], operators[1::2])
        ]
        operators = joined + operators[len(operators) // 2 * 2 :]

    for block in blocks[:-1]:
        moved, cosine, sine = operators[0][block]
        reach = lane + moved.astype(jnp.int32)
        lanes = slice(block * LANES, (block + 1) * LANES)
        index_ref[0, :, lanes] = reach & (LANES - 1)
        index_ref[1, :, lanes] = reach - LANES
        trig_ref[0, :, lanes] = cosine
        trig_ref[1, :, lanes] = sine


def combination(index_ref, trig_ref, row, lanes, rows):
    def spread(values):
        return jnp.broadcast_to(values, (rows, LANES))

    index = spread(index_ref[0, row : row + 1, lanes])
    beyond = spread(index_ref[1, row : row + 1, lanes]) >= 0
    cosine = spread(trig_ref[0, row : row + 1, lanes])
    sine = spread(trig_ref[1, row : row + 1, lanes])
    return index, beyond, cosine, sine


def term_of(here, following, steering):
    index, beyond, cosine, sine = steering
    real, imag = (picked(a, b, index, beyond) for a, b in zip(here, following))
    return real * cosine - imag * sine, real * sine + imag * cosine


def sums_and_differences(values):
    values = list(values)
    distance = 1
    while distance < len(values):
        for at in range(len(values)):
            if not at & distance:
                low, high = values[at], values[at + distance]
                values[at], values[at + distance] = low + high, low - high
        distance *= 2
    return values


def filter_block(tiles, table_ref):
    parts = [
        lax.dot_general(
            jnp.concatenate(tiles[part], axis=1),
            table_ref[part],
            (((1,), (1,)), ((), ())),
            preferred_element_type=F32,
        )
        for part in range(2)
    ]
    return parts[0] + parts[1]


def merge_first(
    levels,
    field_ref,
    here_lanes,
    next_lanes,
    lanes,
    index_ref,
    trig_ref,
    term_ref,
    out_ref,
    out_lanes,
):
    pulses = field_ref.shape[1]
    combinations = 1 << levels
    chunk = pulses // combinations
    for at in range(combinations):
        steering = combination(index_ref, trig_ref, at, lanes, chunk)
        rows = slice(at * chunk, (at + 1) * chunk)
        here = [field_ref[part, rows, here_lanes] for part in range(2)]
        following = [field_ref[part, rows, next_lanes] for part in range(2)]
        term_ref[0, at], term_ref[1, at] = term_of(here, following, steering)
    for tile in range(chunk // 8):
        cut = slice(8 * tile, 8 * tile + 8)
        real, imag = (
            sums_and_differences([term_ref[part, at, cut] for at in range(combinations)])
            for part in range(2)
        )
        for at in range(combinations):
            out_ref[at * (chunk // 8) + tile, :, out_lanes] = jnp.concatenate(
                [real[at], imag[at]], axis=0
            ).astype(BF16)


def inner_merges_kernel(
    inner_levels,
    raw_ref,
    chirp_ref,
    offset_ref,
    phase_ref,
    out_ref,
    ends_ref,
    steering_ref,
    table_ref,
    stored,
    merged_ref,
    field_ref,
    term_ref,
    index_ref,
    trig_ref,
    rows_ref,
):
    tiles = raw_ref.shape[2] // LANES
    levels = offset_ref.shape[0]
    offsets, angles = (by_side(ref, slice(None)) for ref in (offset_ref, phase_ref))
    values = (offsets.astype(F32) + (STEP - 4.0), *scaled_trig(angles))
    for part in range(3):
        steering_ref[part] = values[part]
    blank = jnp.zeros((2 * levels, LANES), F32)
    align(
        [jnp.concatenate([blank, value, blank], axis=1) for value in values],
        inner_levels,
        range(tiles + 1),
        rows_ref,
    )
    steer(levels, inner_levels, range(1, tiles), rows_ref, index_ref, trig_ref)
    fill_toeplitz(chirp_ref, table_ref)
    for block in range(1, tiles):
        cut = slice((block - 1) * LANES, (block + 1) * LANES)
        both = filter_block([[raw_ref[part, :, cut]] for part in range(2)], table_ref)
        lanes = slice(block * LANES, (block + 1) * LANES)
        for part in range(2):
            values = both[:, part * LANES : (part + 1) * LANES]
            field_ref[part, :, lanes] = values
            if block == 1:
                ends_ref[part, :, :LANES] = values
            if block == tiles - 1:
                ends_ref[part, :, LANES:] = values

    def stored_block(lanes):
        return pltpu.make_async_copy(
            merged_ref.at[:, :, lanes], out_ref.at[:, :, lanes], stored.at[0]
        )

    def merge_pair(pair, carry):
        for slot in range(2):
            block = 1 + 2 * pair + slot
            lanes, beyond = at_block(block), at_block(block + 1)
            merge_first(
                inner_levels,
                field_ref,
                lanes,
                beyond,
                lanes,
                index_ref,
                trig_ref,
                term_ref.at[slot],
                merged_ref,
                lanes,
            )
        both = pl.multiple_of((1 + 2 * pair) * LANES, LANES)
        stored_block(pl.ds(both, 2 * LANES)).start()
        return carry

    lax.fori_loop(0, (tiles - 2) // 2, merge_pair, 0)
    stored_block(pl.ds(LANES, (tiles - 2) * LANES)).wait()


def outer_merges_kernel(
    inner_levels,
    total,
    partial_ref,
    ends_ref,
    steering_ref,
    raw_ref,
    paired_ref,
    crossed_ref,
    table_ref,
    out_ref,
    semaphore,
    merged_ref,
    field_ref,
    term_ref,
    index_ref,
    trig_ref,
    rows_ref,
):
    pulses, width = raw_ref.shape[1], raw_ref.shape[2]
    tiles = width // LANES
    rim_rows = steering_ref.shape[1]
    levels = rim_rows // 2
    start = lax.axis_index("rg") * width - LEAD
    odd = lax.rem(lax.axis_index("rg"), 2) == 1

    def left_rim(rows):
        return jnp.where(odd, paired_ref[rows, :], crossed_ref[rows, :])

    def right_rim(rows):
        return jnp.where(odd, crossed_ref[rows, :], paired_ref[rows, :])

    def held(position):
        return slice(position * LANES, (position + 1) * LANES)

    for rim_of, at, near_lanes, blocks in (
        (left_rim, -LANES, slice(0, 2 * LANES), (0, 1)),
        (right_rim, width, slice(width - 2 * LANES, width), (tiles - 1, tiles)),
    ):
        offsets, high, middle, low = (
            rim_of(slice(2 * pulses + k * rim_rows, 2 * pulses + (k + 1) * rim_rows)).astype(F32)
            for k in range(4)
        )
        cosine, sine = scaled_trig(high + middle + low)
        bins = lax.axis_index("rg") * width + at + lax.broadcasted_iota(
            jnp.int32, (rim_rows, LANES), 1
        )
        inside = (bins >= 0) & (bins < total)
        rim = (
            offsets + (STEP - 4.0),
            jnp.where(inside, cosine, 0.0),
            jnp.where(inside, sine, 0.0),
        )
        middle = [steering_ref[part, :, near_lanes] for part in range(3)]
        joined = [
            jnp.concatenate((a, b) if at < 0 else (b, a), axis=1) for a, b in zip(rim, middle)
        ]
        align(joined, inner_levels, blocks, rows_ref)
        steer(levels, inner_levels, blocks, rows_ref, index_ref, trig_ref)

    for position, block in ((0, 0), (3, tiles)):
        pair = []
        for part in range(2):
            rows = slice(part * pulses, (part + 1) * pulses)
            if block == 0:
                pair.append([left_rim(rows), raw_ref[part, :, :LANES]])
            else:
                pair.append([raw_ref[part, :, width - LANES :], right_rim(rows)])
        both = filter_block(pair, table_ref)
        bins = start + block * LANES + (lax.broadcasted_iota(jnp.int32, both.shape, 1) % LANES)
        both = jnp.where((bins >= 0) & (bins < total), both, 0.0)
        for part in range(2):
            field_ref[part, :, held(position)] = both[:, part * LANES : (part + 1) * LANES]
    for part in range(2):
        field_ref[part, :, LANES : 3 * LANES] = ends_ref[part]
    copies = []
    for here, following, block in ((0, 1, 0), (2, 3, tiles - 1)):
        merge_first(
            inner_levels,
            field_ref,
            held(here),
            held(following),
            slice(block * LANES, (block + 1) * LANES),
            index_ref,
            trig_ref,
            term_ref.at[len(copies)],
            merged_ref.at[len(copies)],
            slice(0, LANES),
        )
        copy = pltpu.make_async_copy(
            merged_ref.at[len(copies)],
            out_ref.at[:, :, pl.ds(block * LANES, LANES)],
            semaphore.at[len(copies)],
        )
        copy.start()
        copies.append(copy)
    for copy in copies:
        copy.wait()


def last_sums_kernel(target_ref, moved_ref, out_ref, term_ref):
    holders, rows, columns = moved_ref.shape
    per_tile = out_ref.shape[2] // LANES
    tiles_across = columns // out_ref.shape[2]
    near_group = min(8, holders)
    for column in range(tiles_across):
        for part in range(per_tile):
            start = (column * per_tile + part) * LANES
            lanes = slice(start, start + LANES)
            inner = slice(part * LANES, (part + 1) * LANES)
            for first in range(0, holders, near_group):
                sums = sums_and_differences(
                    [moved_ref[first + at, :, lanes].astype(F32) for at in range(near_group)]
                )
                for at in range(near_group):
                    term_ref[part, first + at] = sums[at]
            for first in range(near_group):
                members = range(first, holders, near_group)
                sums = sums_and_differences([term_ref[part, at] for at in members])
                for at, value in zip(members, sums):
                    to = target_ref[at * tiles_across + column]
                    out_ref[to, :, inner] = value.astype(BF16)


def place_kernel(steps, source_ref, incoming_ref, out_ref, image_ref, semaphore):
    _, rows, width = out_ref.shape
    tile_bins = incoming_ref.shape[2]
    across = width // tile_bins
    share = rows // steps
    copies = []
    for step in range(steps):
        for row in range(step * share // 8, (step + 1) * share // 8):
            for column in range(across):
                tile = incoming_ref[source_ref[row * across + column]].astype(F32)
                for part in range(2):
                    image_ref[
                        part, row * 8 : row * 8 + 8, column * tile_bins : (column + 1) * tile_bins
                    ] = tile[8 * part : 8 * part + 8]
        cut = pl.ds(step * share, share)
        copy = pltpu.make_async_copy(
            image_ref.at[:, cut, :], out_ref.at[:, cut, :], semaphore.at[step]
        )
        copy.start()
        copies.append(copy)
    for copy in copies:
        copy.wait()


def per_device(raw_echoes, chirp, range_offsets, phases, tile_table):
    ap_count, rg_count = lax.axis_size("ap"), lax.axis_size("rg")
    devices = ap_count * rg_count
    _, pulses, width = raw_echoes.shape
    level_count = range_offsets.shape[0]
    total = width * rg_count
    outer_levels = ap_count.bit_length() - 1
    inner_levels = level_count - outer_levels
    tile_rows = pulses // ap_count
    tile_bins = width // rg_count
    rim_rows = 2 * pulses + 8 * level_count
    shape = jax.ShapeDtypeStruct

    anywhere = pl.BlockSpec(memory_space=pl.ANY)
    distant = pl.BlockSpec(memory_space=pltpu.HBM)
    to_paired, to_crossed, near_chirp, near_offsets, near_phases, near_raw = pl.pallas_call(
        rim_kernel,
        out_shape=[VMEM((rim_rows, LANES), BF16)] * 2
        + [
            VMEM(chirp.shape, F32),
            VMEM(range_offsets.shape, jnp.int32),
            VMEM(phases.shape, F32),
            VMEM(raw_echoes.shape, BF16),
        ],
        compiler_params=params(),
        in_specs=[distant] * 4,
        out_specs=whole(6),
        scratch_shapes=[pltpu.SemaphoreType.DMA((8,))],
    )(*map(far, (raw_echoes, chirp, range_offsets, phases)))
    from_paired = lax.ppermute(to_paired, "rg", [(i, i ^ 1) for i in range(rg_count)])
    crossed_pairs = [(i, i + 1) for i in range(1, rg_count - 1, 2)]
    from_crossed = lax.ppermute(
        to_crossed, "rg", crossed_pairs + [(j, i) for i, j in crossed_pairs]
    )
    inner = 1 << inner_levels
    merged_shape = pltpu.HBM((ap_count, 2 * tile_rows, width), BF16)

    def first_scratch(held):
        return [
            VMEM((2, pulses, held), F32),
            VMEM((2, 2, inner, pulses // inner, LANES), F32),
            VMEM((2, inner, width), jnp.int32),
            VMEM((2, inner, width), F32),
            VMEM((3, 3 * level_count, width + LANES), F32),
        ]

    partial, field_ends, steering, table = pl.pallas_call(
        functools.partial(inner_merges_kernel, inner_levels),
        out_shape=[
            merged_shape,
            VMEM((2, pulses, 2 * LANES), F32),
            VMEM((3, 2 * level_count, width), F32),
            VMEM((2, 2 * LANES, 2 * LANES), BF16),
        ],
        compiler_params=params(),
        in_specs=whole(4),
        out_specs=[distant] + whole(3),
        scratch_shapes=[
            pltpu.SemaphoreType.DMA((1,)),
            VMEM((ap_count, 2 * tile_rows, width), BF16),
        ]
        + first_scratch(width),
    )(*map(near, (near_raw, near_chirp, near_offsets, near_phases)))
    merged = pl.pallas_call(
        functools.partial(outer_merges_kernel, inner_levels, total),
        out_shape=merged_shape,
        compiler_params=params(),
        in_specs=[distant] + whole(6),
        out_specs=distant,
        input_output_aliases={0: 0},
        scratch_shapes=[
            pltpu.SemaphoreType.DMA((2,)),
            VMEM((2, ap_count, 2 * tile_rows, LANES), BF16),
        ]
        + first_scratch(4 * LANES),
    )(
        far(partial),
        *map(near, (field_ends, steering, near_raw, from_paired, from_crossed, table)),
    )
    moved = lax.all_to_all(merged, "ap", split_axis=0, concat_axis=0, tiled=True)

    ap_here, rg_here = lax.axis_index("ap"), lax.axis_index("rg")
    slot_row = tile_table // (rg_count * rg_count)
    slot_col = tile_table % (rg_count * rg_count)
    target = slot_row // ap_count * rg_count + slot_col // rg_count
    shaped = (ap_count, ap_count, rg_count, rg_count)
    target = target.reshape(shaped)
    local_slot = (slot_row % ap_count * rg_count + slot_col % rg_count).reshape(shaped)
    mine = target == ap_here * rg_count + rg_here
    slot_from = jnp.sum(jnp.where(mine, local_slot, 0), axis=(0, 3)).reshape(devices)
    ids = jnp.arange(devices, dtype=jnp.int32)
    source = jnp.sum(
        jnp.where(slot_from[None, :] == ids[:, None], ids[None, :], 0), axis=1
    )
    send_to = lax.dynamic_slice(
        target, (0, ap_here, rg_here, 0), (ap_count, 1, 1, rg_count)
    ).reshape(devices)

    moved, source = lax.optimization_barrier((moved, source))
    outgoing = pl.pallas_call(
        last_sums_kernel,
        out_shape=VMEM((devices, 2 * tile_rows, tile_bins), BF16),
        compiler_params=params(),
        grid_spec=pltpu.PrefetchScalarGridSpec(
            num_scalar_prefetch=1,
            in_specs=whole(1),
            out_specs=whole(1)[0],
            scratch_shapes=[VMEM((tile_bins // LANES, ap_count, 2 * tile_rows, LANES), F32)],
        ),
    )(send_to, near(moved))
    incoming = lax.all_to_all(outgoing, ("ap", "rg"), split_axis=0, concat_axis=0, tiled=True)
    steps = 8
    return pl.pallas_call(
        functools.partial(place_kernel, steps),
        out_shape=shape((2, pulses, width), F32),
        compiler_params=params(),
        grid_spec=pltpu.PrefetchScalarGridSpec(
            num_scalar_prefetch=1,
            in_specs=whole(1),
            out_specs=anywhere,
            scratch_shapes=[VMEM((2, pulses, width), F32), pltpu.SemaphoreType.DMA((steps,))],
        ),
    )(source, near(incoming))


def solution(mesh):
    placed = (P(None, "ap", "rg"), P(), P(None, None, "rg"), P(None, None, "rg"), P())
    return jax.shard_map(
        per_device, mesh=mesh, in_specs=placed, out_specs=P(None, "ap", "rg"), check_vma=False
    )
```

```python
import functools
import math

import jax
import jax.numpy as jnp
from jax import lax
from jax.experimental import pallas as pl
from jax.experimental.pallas import tpu as pltpu
from jax.sharding import PartitionSpec as P

ROOT_HALF = 0.7071067811865476
LANES = 128
STEP = 8
LEAD = 64
VMEM = pltpu.VMEM
BF16 = jnp.bfloat16
F32 = jnp.float32


def whole(count):
    return [pl.BlockSpec(memory_space=VMEM)] * count


def near(value):
    return pltpu.with_memory_space_constraint(value, VMEM)


def far(value):
    return pltpu.with_memory_space_constraint(value, pltpu.HBM)


def params():
    return pltpu.CompilerParams(vmem_limit_bytes=24 * 2**20)


def at_block(block):
    return pl.ds(pl.multiple_of(block * LANES, LANES), LANES)


def split_three(values):
    high = values.astype(BF16)
    rest = values - high.astype(F32)
    middle = rest.astype(BF16)
    low = (rest - middle.astype(F32)).astype(BF16)
    return high, middle, low


def rim_kernel(
    raw_ref,
    chirp_ref,
    offset_ref,
    phase_ref,
    paired_ref,
    crossed_ref,
    near_chirp,
    near_offset,
    near_phase,
    near_raw,
    semaphore,
):
    _, pulses, width = raw_ref.shape
    far_end = width - LANES
    odd = lax.rem(lax.axis_index("rg"), 2)
    paired_at = pl.multiple_of((1 - odd) * far_end, LANES)
    crossed_at = pl.multiple_of(odd * far_end, LANES)
    levels = offset_ref.shape[0]
    rows = 2 * levels
    copies = []
    for source, target in (
        (offset_ref, near_offset),
        (phase_ref, near_phase),
        (raw_ref.at[0, :, pl.ds(paired_at, LANES)], paired_ref.at[:pulses]),
        (raw_ref.at[1, :, pl.ds(paired_at, LANES)], paired_ref.at[pulses : 2 * pulses]),
        (raw_ref.at[0, :, pl.ds(crossed_at, LANES)], crossed_ref.at[:pulses]),
        (raw_ref.at[1, :, pl.ds(crossed_at, LANES)], crossed_ref.at[pulses : 2 * pulses]),
        (chirp_ref, near_chirp),
        (raw_ref, near_raw),
    ):
        copy = pltpu.make_async_copy(source, target, semaphore.at[len(copies)])
        copy.start()
        copies.append(copy)
    for copy in copies[:2]:
        copy.wait()
    for start, out_ref in ((paired_at, paired_ref), (crossed_at, crossed_ref)):
        cut = pl.ds(start, LANES)
        at = 2 * pulses
        offsets, angles = by_side(near_offset, cut), by_side(near_phase, cut)
        out_ref[at : at + rows] = offsets.astype(F32).astype(BF16)
        for part in split_three(angles):
            at += rows
            out_ref[at : at + rows] = part
    for copy in copies[2:]:
        copy.wait()


def fill_toeplitz(chirp_ref, table_ref):
    taps = chirp_ref[...].astype(BF16).astype(F32)
    zeros = jnp.zeros((1, LANES), F32)
    rolled = []
    for part in range(2):
        row = jnp.concatenate([taps[part : part + 1], zeros], axis=1)
        spread = jnp.broadcast_to(row, (LANES, 2 * LANES))
        rolled.append(pltpu.roll(spread, 0, 1, stride=1, stride_axis=0))
    real, imag = rolled
    table_ref[0] = jnp.concatenate([real, -imag], axis=0).astype(BF16)
    table_ref[1] = jnp.concatenate([imag, real], axis=0).astype(BF16)


def gathered(values, index):
    return lax.gather(
        values,
        index[:, :, None],
        lax.GatherDimensionNumbers(
            offset_dims=(),
            collapsed_slice_dims=(1,),
            start_index_map=(1,),
            operand_batching_dims=(0,),
            start_indices_batching_dims=(0,),
        ),
        slice_sizes=(1, 1),
        mode=lax.GatherScatterMode.PROMISE_IN_BOUNDS,
    )


def picked(here, following, index, beyond):
    return jnp.where(beyond, gathered(following, index), gathered(here, index))


def scaled_trig(angles):
    return jnp.cos(angles) * ROOT_HALF, jnp.sin(angles) * ROOT_HALF


def by_side(ref, lanes):
    levels = ref.shape[0]
    return jnp.concatenate(
        [ref[level, side : side + 1, lanes] for side in range(2) for level in reversed(range(levels))],
        axis=0,
    )


def align(values, inner_levels, blocks, rows_ref):
    rows, width = values[0].shape
    levels = rows // 2
    lanes = slice(blocks[0] * LANES, (blocks[-1] + 1) * LANES)
    count = len(blocks) * LANES
    level = levels - 1 - lax.broadcasted_iota(jnp.int32, (levels, count), 0)
    bit = jnp.left_shift(1, jnp.maximum(level - inner_levels, 0))
    upper = (lax.axis_index("ap") & bit) != 0
    for part in range(3):
        sides = [
            pltpu.roll(
                values[part][side * levels : (side + 1) * levels],
                width - (LEAD + STEP * levels),
                1,
                stride=STEP,
                stride_axis=0,
            )[:, :count]
            for side in range(2)
        ]
        for at, moved in enumerate(sides + [jnp.where(upper, sides[1], sides[0])]):
            rows_ref[part, at * levels : (at + 1) * levels, lanes] = moved


def compose(outer, inner, inner_beyond, lane):
    step, cos_out, sin_out = outer
    index = lane + step.astype(jnp.int32)
    beyond = index >= LANES
    index = index & (LANES - 1)
    moved, cos_in, sin_in = (
        picked(a, b, index, beyond) for a, b in zip(inner, inner_beyond)
    )
    return (
        step + moved,
        cos_out * cos_in - sin_out * sin_in,
        cos_out * sin_in + sin_out * cos_in,
    )


def steer(levels, inner_levels, blocks, rows_ref, index_ref, trig_ref):
    lane = lax.broadcasted_iota(jnp.int32, (8, LANES), 1)
    last = blocks[-1]

    def row(slot, block):
        lanes = slice(block * LANES, (block + 1) * LANES)
        return tuple(
            jnp.broadcast_to(rows_ref[part, slot : slot + 1, lanes], (8, LANES))
            for part in range(3)
        )

    sublane = lax.broadcasted_iota(jnp.int32, (8, LANES), 0)

    def operator(level):
        slot = levels - 1 - level
        if level >= inner_levels:
            return {block: row(2 * levels + slot, block) for block in blocks}
        upper = ((sublane >> level) & 1) == 1
        return {
            block: tuple(
                jnp.where(upper, b, a)
                for a, b in zip(row(slot, block), row(levels + slot, block))
            )
            for block in blocks
        }

    operators = [operator(level) for level in range(levels)]
    while len(operators) > 1:
        kept = blocks[:-1] if len(operators) == 2 else blocks
        joined = [
            {
                block: compose(outer[block], inner[block], inner[min(block + 1, last)], lane)
                for block in kept
            }
            for inner, outer in zip(operators[0::2], operators[1::2])
        ]
        operators = joined + operators[len(operators) // 2 * 2 :]

    for block in blocks[:-1]:
        moved, cosine, sine = operators[0][block]
        reach = lane + moved.astype(jnp.int32)
        lanes = slice(block * LANES, (block + 1) * LANES)
        index_ref[0, :, lanes] = reach & (LANES - 1)
        index_ref[1, :, lanes] = reach - LANES
        trig_ref[0, :, lanes] = cosine
        trig_ref[1, :, lanes] = sine


def combination(index_ref, trig_ref, row, lanes, rows):
    def spread(values):
        return jnp.broadcast_to(values, (rows, LANES))

    index = spread(index_ref[0, row : row + 1, lanes])
    beyond = spread(index_ref[1, row : row + 1, lanes]) >= 0
    cosine = spread(trig_ref[0, row : row + 1, lanes])
    sine = spread(trig_ref[1, row : row + 1, lanes])
    return index, beyond, cosine, sine


def term_of(here, following, steering):
    index, beyond, cosine, sine = steering
    real, imag = (picked(a, b, index, beyond) for a, b in zip(here, following))
    return real * cosine - imag * sine, real * sine + imag * cosine


def sums_and_differences(values):
    values = list(values)
    distance = 1
    while distance < len(values):
        for at in range(len(values)):
            if not at & distance:
                low, high = values[at], values[at + distance]
                values[at], values[at + distance] = low + high, low - high
        distance *= 2
    return values


def filter_block(tiles, table_ref):
    parts = [
        lax.dot_general(
            jnp.concatenate(tiles[part], axis=1),
            table_ref[part],
            (((1,), (1,)), ((), ())),
            preferred_element_type=F32,
        )
        for part in range(2)
    ]
    return parts[0] + parts[1]


def merge_first(
    levels,
    field_ref,
    here_lanes,
    next_lanes,
    lanes,
    index_ref,
    trig_ref,
    term_ref,
    out_ref,
    out_lanes,
):
    pulses = field_ref.shape[1]
    combinations = 1 << levels
    chunk = pulses // combinations
    for at in range(combinations):
        steering = combination(index_ref, trig_ref, at, lanes, chunk)
        rows = slice(at * chunk, (at + 1) * chunk)
        here = [field_ref[part, rows, here_lanes] for part in range(2)]
        following = [field_ref[part, rows, next_lanes] for part in range(2)]
        term_ref[0, at], term_ref[1, at] = term_of(here, following, steering)
    for tile in range(chunk // 8):
        cut = slice(8 * tile, 8 * tile + 8)
        real, imag = (
            sums_and_differences([term_ref[part, at, cut] for at in range(combinations)])
            for part in range(2)
        )
        for at in range(combinations):
            out_ref[at * (chunk // 8) + tile, :, out_lanes] = jnp.concatenate(
                [real[at], imag[at]], axis=0
            ).astype(BF16)


def inner_merges_kernel(
    inner_levels,
    raw_ref,
    chirp_ref,
    offset_ref,
    phase_ref,
    out_ref,
    ends_ref,
    steering_ref,
    table_ref,
    stored,
    merged_ref,
    field_ref,
    term_ref,
    index_ref,
    trig_ref,
    rows_ref,
):
    tiles = raw_ref.shape[2] // LANES
    levels = offset_ref.shape[0]
    offsets, angles = (by_side(ref, slice(None)) for ref in (offset_ref, phase_ref))
    values = (offsets.astype(F32) + (STEP - 4.0), *scaled_trig(angles))
    for part in range(3):
        steering_ref[part] = values[part]
    blank = jnp.zeros((2 * levels, LANES), F32)
    align(
        [jnp.concatenate([blank, value, blank], axis=1) for value in values],
        inner_levels,
        range(tiles + 1),
        rows_ref,
    )
    steer(levels, inner_levels, range(1, tiles), rows_ref, index_ref, trig_ref)
    fill_toeplitz(chirp_ref, table_ref)
    for block in range(1, tiles):
        cut = slice((block - 1) * LANES, (block + 1) * LANES)
        both = filter_block([[raw_ref[part, :, cut]] for part in range(2)], table_ref)
        lanes = slice(block * LANES, (block + 1) * LANES)
        for part in range(2):
            values = both[:, part * LANES : (part + 1) * LANES]
            field_ref[part, :, lanes] = values
            if block == 1:
                ends_ref[part, :, :LANES] = values
            if block == tiles - 1:
                ends_ref[part, :, LANES:] = values

    def stored_block(lanes):
        return pltpu.make_async_copy(
            merged_ref.at[:, :, lanes], out_ref.at[:, :, lanes], stored.at[0]
        )

    def merge_pair(pair, carry):
        for slot in range(2):
            block = 1 + 2 * pair + slot
            lanes, beyond = at_block(block), at_block(block + 1)
            merge_first(
                inner_levels,
                field_ref,
                lanes,
                beyond,
                lanes,
                index_ref,
                trig_ref,
                term_ref.at[slot],
                merged_ref,
                lanes,
            )
        both = pl.multiple_of((1 + 2 * pair) * LANES, LANES)
        stored_block(pl.ds(both, 2 * LANES)).start()
        return carry

    lax.fori_loop(0, (tiles - 2) // 2, merge_pair, 0)
    stored_block(pl.ds(LANES, (tiles - 2) * LANES)).wait()


def outer_merges_kernel(
    inner_levels,
    total,
    partial_ref,
    ends_ref,
    steering_ref,
    raw_ref,
    paired_ref,
    crossed_ref,
    table_ref,
    out_ref,
    semaphore,
    merged_ref,
    field_ref,
    term_ref,
    index_ref,
    trig_ref,
    rows_ref,
):
    pulses, width = raw_ref.shape[1], raw_ref.shape[2]
    tiles = width // LANES
    rim_rows = steering_ref.shape[1]
    levels = rim_rows // 2
    start = lax.axis_index("rg") * width - LEAD
    odd = lax.rem(lax.axis_index("rg"), 2) == 1

    def left_rim(rows):
        return jnp.where(odd, paired_ref[rows, :], crossed_ref[rows, :])

    def right_rim(rows):
        return jnp.where(odd, crossed_ref[rows, :], paired_ref[rows, :])

    def held(position):
        return slice(position * LANES, (position + 1) * LANES)

    for rim_of, at, near_lanes, blocks in (
        (left_rim, -LANES, slice(0, 2 * LANES), (0, 1)),
        (right_rim, width, slice(width - 2 * LANES, width), (tiles - 1, tiles)),
    ):
        offsets, high, middle, low = (
            rim_of(slice(2 * pulses + k * rim_rows, 2 * pulses + (k + 1) * rim_rows)).astype(F32)
            for k in range(4)
        )
        cosine, sine = scaled_trig(high + middle + low)
        bins = lax.axis_index("rg") * width + at + lax.broadcasted_iota(
            jnp.int32, (rim_rows, LANES), 1
        )
        inside = (bins >= 0) & (bins < total)
        rim = (
            offsets + (STEP - 4.0),
            jnp.where(inside, cosine, 0.0),
            jnp.where(inside, sine, 0.0),
        )
        middle = [steering_ref[part, :, near_lanes] for part in range(3)]
        joined = [
            jnp.concatenate((a, b) if at < 0 else (b, a), axis=1) for a, b in zip(rim, middle)
        ]
        align(joined, inner_levels, blocks, rows_ref)
        steer(levels, inner_levels, blocks, rows_ref, index_ref, trig_ref)

    for position, block in ((0, 0), (3, tiles)):
        pair = []
        for part in range(2):
            rows = slice(part * pulses, (part + 1) * pulses)
            if block == 0:
                pair.append([left_rim(rows), raw_ref[part, :, :LANES]])
            else:
                pair.append([raw_ref[part, :, width - LANES :], right_rim(rows)])
        both = filter_block(pair, table_ref)
        bins = start + block * LANES + (lax.broadcasted_iota(jnp.int32, both.shape, 1) % LANES)
        both = jnp.where((bins >= 0) & (bins < total), both, 0.0)
        for part in range(2):
            field_ref[part, :, held(position)] = both[:, part * LANES : (part + 1) * LANES]
    for part in range(2):
        field_ref[part, :, LANES : 3 * LANES] = ends_ref[part]
    copies = []
    for here, following, block in ((0, 1, 0), (2, 3, tiles - 1)):
        merge_first(
            inner_levels,
            field_ref,
            held(here),
            held(following),
            slice(block * LANES, (block + 1) * LANES),
            index_ref,
            trig_ref,
            term_ref.at[len(copies)],
            merged_ref.at[len(copies)],
            slice(0, LANES),
        )
        copy = pltpu.make_async_copy(
            merged_ref.at[len(copies)],
            out_ref.at[:, :, pl.ds(block * LANES, LANES)],
            semaphore.at[len(copies)],
        )
        copy.start()
        copies.append(copy)
    for copy in copies:
        copy.wait()


def last_sums_kernel(target_ref, moved_ref, out_ref, term_ref):
    holders, rows, columns = moved_ref.shape
    per_tile = out_ref.shape[2] // LANES
    tiles_across = columns // out_ref.shape[2]
    near_group = min(4, holders)
    for column in range(tiles_across):
        for part in range(per_tile):
            start = (column * per_tile + part) * LANES
            lanes = slice(start, start + LANES)
            inner = slice(part * LANES, (part + 1) * LANES)
            for first in range(0, holders, near_group):
                sums = sums_and_differences(
                    [moved_ref[first + at, :, lanes].astype(F32) for at in range(near_group)]
                )
                for at in range(near_group):
                    term_ref[part, first + at] = sums[at]
            for first in range(near_group):
                members = range(first, holders, near_group)
                sums = sums_and_differences([term_ref[part, at] for at in members])
                for at, value in zip(members, sums):
                    to = target_ref[at * tiles_across + column]
                    out_ref[to, :, inner] = value.astype(BF16)


def place_kernel(steps, source_ref, incoming_ref, out_ref, image_ref, semaphore):
    _, rows, width = out_ref.shape
    tile_bins = incoming_ref.shape[2]
    across = width // tile_bins
    share = rows // steps
    copies = []
    for step in range(steps):
        for row in range(step * share // 8, (step + 1) * share // 8):
            for column in range(across):
                tile = incoming_ref[source_ref[row * across + column]].astype(F32)
                for part in range(2):
                    image_ref[
                        part, row * 8 : row * 8 + 8, column * tile_bins : (column + 1) * tile_bins
                    ] = tile[8 * part : 8 * part + 8]
        cut = pl.ds(step * share, share)
        copy = pltpu.make_async_copy(
            image_ref.at[:, cut, :], out_ref.at[:, cut, :], semaphore.at[step]
        )
        copy.start()
        copies.append(copy)
    for copy in copies:
        copy.wait()


def per_device(raw_echoes, chirp, range_offsets, phases, tile_table):
    ap_count, rg_count = lax.axis_size("ap"), lax.axis_size("rg")
    devices = ap_count * rg_count
    _, pulses, width = raw_echoes.shape
    level_count = range_offsets.shape[0]
    total = width * rg_count
    outer_levels = ap_count.bit_length() - 1
    inner_levels = level_count - outer_levels
    tile_rows = pulses // ap_count
    tile_bins = width // rg_count
    rim_rows = 2 * pulses + 8 * level_count
    shape = jax.ShapeDtypeStruct

    anywhere = pl.BlockSpec(memory_space=pl.ANY)
    distant = pl.BlockSpec(memory_space=pltpu.HBM)
    to_paired, to_crossed, near_chirp, near_offsets, near_phases, near_raw = pl.pallas_call(
        rim_kernel,
        out_shape=[VMEM((rim_rows, LANES), BF16)] * 2
        + [
            VMEM(chirp.shape, F32),
            VMEM(range_offsets.shape, jnp.int32),
            VMEM(phases.shape, F32),
            VMEM(raw_echoes.shape, BF16),
        ],
        compiler_params=params(),
        in_specs=[distant] * 4,
        out_specs=whole(6),
        scratch_shapes=[pltpu.SemaphoreType.DMA((8,))],
    )(*map(far, (raw_echoes, chirp, range_offsets, phases)))
    from_paired = lax.ppermute(to_paired, "rg", [(i, i ^ 1) for i in range(rg_count)])
    crossed_pairs = [(i, i + 1) for i in range(1, rg_count - 1, 2)]
    from_crossed = lax.ppermute(
        to_crossed, "rg", crossed_pairs + [(j, i) for i, j in crossed_pairs]
    )
    inner = 1 << inner_levels
    merged_shape = pltpu.HBM((ap_count, 2 * tile_rows, width), BF16)

    def first_scratch(held):
        return [
            VMEM((2, pulses, held), F32),
            VMEM((2, 2, inner, pulses // inner, LANES), F32),
            VMEM((2, inner, width), jnp.int32),
            VMEM((2, inner, width), F32),
            VMEM((3, 3 * level_count, width + LANES), F32),
        ]

    partial, field_ends, steering, table = pl.pallas_call(
        functools.partial(inner_merges_kernel, inner_levels),
        out_shape=[
            merged_shape,
            VMEM((2, pulses, 2 * LANES), F32),
            VMEM((3, 2 * level_count, width), F32),
            VMEM((2, 2 * LANES, 2 * LANES), BF16),
        ],
        compiler_params=params(),
        in_specs=whole(4),
        out_specs=[distant] + whole(3),
        scratch_shapes=[
            pltpu.SemaphoreType.DMA((1,)),
            VMEM((ap_count, 2 * tile_rows, width), BF16),
        ]
        + first_scratch(width),
    )(*map(near, (near_raw, near_chirp, near_offsets, near_phases)))
    merged = pl.pallas_call(
        functools.partial(outer_merges_kernel, inner_levels, total),
        out_shape=merged_shape,
        compiler_params=params(),
        in_specs=[distant] + whole(6),
        out_specs=distant,
        input_output_aliases={0: 0},
        scratch_shapes=[
            pltpu.SemaphoreType.DMA((2,)),
            VMEM((2, ap_count, 2 * tile_rows, LANES), BF16),
        ]
        + first_scratch(4 * LANES),
    )(
        far(partial),
        *map(near, (field_ends, steering, near_raw, from_paired, from_crossed, table)),
    )
    moved = lax.all_to_all(merged, "ap", split_axis=0, concat_axis=0, tiled=True)

    ap_here, rg_here = lax.axis_index("ap"), lax.axis_index("rg")
    slot_row = tile_table // (rg_count * rg_count)
    slot_col = tile_table % (rg_count * rg_count)
    target = slot_row // ap_count * rg_count + slot_col // rg_count
    shaped = (ap_count, ap_count, rg_count, rg_count)
    target = target.reshape(shaped)
    local_slot = (slot_row % ap_count * rg_count + slot_col % rg_count).reshape(shaped)
    mine = target == ap_here * rg_count + rg_here
    slot_from = jnp.sum(jnp.where(mine, local_slot, 0), axis=(0, 3)).reshape(devices)
    ids = jnp.arange(devices, dtype=jnp.int32)
    source = jnp.sum(
        jnp.where(slot_from[None, :] == ids[:, None], ids[None, :], 0), axis=1
    )
    send_to = lax.dynamic_slice(
        target, (0, ap_here, rg_here, 0), (ap_count, 1, 1, rg_count)
    ).reshape(devices)

    moved, source = lax.optimization_barrier((moved, source))
    outgoing = pl.pallas_call(
        last_sums_kernel,
        out_shape=VMEM((devices, 2 * tile_rows, tile_bins), BF16),
        compiler_params=params(),
        grid_spec=pltpu.PrefetchScalarGridSpec(
            num_scalar_prefetch=1,
            in_specs=whole(1),
            out_specs=whole(1)[0],
            scratch_shapes=[VMEM((tile_bins // LANES, ap_count, 2 * tile_rows, LANES), F32)],
        ),
    )(send_to, near(moved))
    incoming = lax.all_to_all(outgoing, ("ap", "rg"), split_axis=0, concat_axis=0, tiled=True)
    steps = 16
    return pl.pallas_call(
        functools.partial(place_kernel, steps),
        out_shape=shape((2, pulses, width), F32),
        compiler_params=params(),
        grid_spec=pltpu.PrefetchScalarGridSpec(
            num_scalar_prefetch=1,
            in_specs=whole(1),
            out_specs=anywhere,
            scratch_shapes=[VMEM((2, pulses, width), F32), pltpu.SemaphoreType.DMA((steps,))],
        ),
    )(source, near(incoming))


def solution(mesh):
    placed = (P(None, "ap", "rg"), P(), P(None, None, "rg"), P(None, None, "rg"), P())
    return jax.shard_map(
        per_device, mesh=mesh, in_specs=placed, out_specs=P(None, "ap", "rg"), check_vma=False
    )
```
